256 devices in a mesh: rep: 16 (over z, y_hi), ep: 16 (over x, y_lo, core).
Axes of the slice: x: 4, y: 4 (y_hi: 2, y_lo: 2; y = y_hi * 2 + y_lo), z: 8, core: 2. Of those that a mesh axis runs over, the one named last changes fastest.
Arguments:
- tokens: bfloat16 [8192, 7168], P(('rep', 'ep')), may hold values from -6 to 6
- routes: int32 [8192, 2], P(('rep', 'ep')), may hold values from 0 to 7, all different within a row; in each aligned block of 32 rows (0 to 31, 32 to 63, ...) at most 16 rows name the same one
- gates: float32 [8192, 2], P(('rep', 'ep')), may hold values from 0.2 to 1
- gate_weight: bfloat16 [8192, 7168], P('ep', 'rep'), may hold values from -0.0625 to 0.0625
- up_weight: bfloat16 [8192, 7168], P('ep', 'rep'), may hold values from -0.0625 to 0.0625
- down_weight: bfloat16 [8192, 7168], P('ep', 'rep'), may hold values from -0.1875 to 0.1875
Outputs:
- combined: bfloat16 [8192, 7168], P(('rep', 'ep'))
The draws below stay inside these ranges and needn't reach their ends.
Inputs may be any that keep to these rules, and one draw needn't show every extreme that they name: `routes`: A row names 2 different experts; in each aligned block of 32 rows (the rows of one device) no expert is named by more than 16 rows, a bound that some block reaches.
All inputs are finite; a program needn't handle non-finite values.
Results may differ from the reference program's by a relative error of at most 0.0065.
Values may be sent and summed in bfloat16 or wider, within the bound.
A program may use at most 128 MiB of HBM per device.

```python
import math
import jax
import jax.numpy as jnp
import numpy as np
from jax import lax

D = 7168
H = 1024
TOK_DEV = 32
EXPERTS = 8
TOP = 2
CAP = 16
TOKENS = 8192


def block_scale(rng, dims, split, smallest, high):
    level, own = 1.0, jax.random.fold_in(rng, 6)
    for axis_at, parts in split:
        draws = jnp.exp(jax.random.uniform(jax.random.fold_in(own, axis_at), (parts,), jnp.float32, smallest / len(split), high / len(split)))
        level = level * jnp.repeat(draws, dims[axis_at] // parts).reshape([-1 if axis == axis_at else 1 for axis in range(len(dims))])
    return level


def deal_out(stream_key, own, number, rows, count, top, bound, skew):
    sequence = jax.random.permutation(stream_key, count)
    heavy_load, usual = portions_of(count, rows * top, bound, skew, True), portions_of(count, rows * top, bound, skew, False)
    places = jnp.arange(count)

    def named(sizes, rotation):
        used = int((sizes > 0).sum())
        fixed = max(1, used // 4)
        shifted = fixed + (places - fixed + rotation * (used - fixed)) % max(1, count - fixed)
        return jnp.zeros((count,), jnp.int32).at[sequence[jnp.where(places < fixed, places, shifted)]].set(jnp.asarray(sizes, jnp.int32))

    sizes = jnp.where(number % 4 == 0, named(heavy_load, number // 4), named(usual, number - number // 4 - 1))
    mixed = jax.random.permutation(jax.random.fold_in(own, 3), count)
    giver, taker = mixed[0:count // 2 * 2:2], mixed[1:count // 2 * 2:2]
    slack = jnp.minimum(sizes[giver] - 1, bound - sizes[taker]) // 2
    slack = jnp.where((giver == sequence[0]) | (taker == sequence[0]) | (sizes[taker] == 0), 0, jnp.maximum(slack, 0))
    shifted = jax.random.randint(jax.random.fold_in(own, 4), (count // 2,), 0, 1 << 20) % (slack + 1)
    sizes = sizes.at[giver].add(-shifted).at[taker].add(shifted)
    items = jnp.searchsorted(jnp.cumsum(sizes), jnp.arange(rows * top), side="right").astype(jnp.int32)
    listing = items.reshape(top, rows).T
    listing = listing[jax.random.permutation(jax.random.fold_in(own, 1), rows)]
    rotation = jax.random.randint(jax.random.fold_in(own, 2), (rows, 1), 0, top)
    return jnp.take_along_axis(listing, (jnp.arange(top)[None, :] + rotation) % top, axis=1)


def portions_of(count, total, reach, skew, full):
    portions = [(1 << 20) // math.isqrt(grade ** skew) + 1 for grade in range(1, count + 1)]
    largest = reach if full else min(reach, max(-(-total // count), total * portions[0] // sum(portions)))
    least = 1 if total - largest >= count - 1 else 0
    counts, rest = [largest] + [least] * (count - 1), total - largest - least * (count - 1)
    while rest > 0:
        movable = [i for i in range(1, count) if counts[i] < largest] or [i for i in range(1, count) if counts[i] < reach]
        whole, remaining = sum([portions[i] for i in movable]), rest
        for i in movable:
            addition = min(reach - counts[i], max(1, remaining * portions[i] // whole), rest)
            counts[i] = counts[i] + addition
            rest = rest - addition
    return np.array(counts)


def scatter_about(stream_key, shape, width, most, shards=(), kind=jnp.bfloat16):
    gain = block_scale(stream_key, shape, shards, -0.22, 0.18) if shards else 1.0
    values = jax.random.normal(stream_key, shape, jnp.float32) * width * gain
    return jnp.minimum(jnp.maximum(values, -most), most).astype(kind)


def setup_inputs(seed: int = 0) -> dict:
    seeds = jax.random.split(jax.random.key(seed), 7)
    tokens = scatter_about(seeds[0], (TOKENS, D), 1.0, 6.0, ((0, 256),))
    routes_keys = jax.random.split(jax.random.fold_in(seeds[1], 1), TOKENS // TOK_DEV)
    routes_turns = jax.random.permutation(jax.random.fold_in(seeds[1], 3), TOKENS // TOK_DEV)
    routes = jax.vmap(lambda own, number: deal_out(jax.random.fold_in(seeds[1], 2), own, number, TOK_DEV, EXPERTS, TOP, CAP, 2))(routes_keys, routes_turns).reshape((TOKENS, TOP))
    gates = jnp.clip(0.2 + 0.8 * jax.random.uniform(seeds[2], (TOKENS, TOP), jnp.float32) ** block_scale(seeds[2], (TOKENS, TOP), ((0, 256),), -0.2, 0.2), 0.2, 1.0)
    gate_weight = scatter_about(seeds[3], (EXPERTS * H, D), D ** -0.5, 0.0625, ((0, 16), (1, 16)))
    up_weight = scatter_about(seeds[4], (EXPERTS * H, D), D ** -0.5, 0.0625, ((0, 16), (1, 16)))
    down_weight = scatter_about(seeds[5], (EXPERTS * H, D), H ** -0.5, 0.1875, ((0, 16), (1, 16)))
    return dict(tokens=tokens, routes=routes, gates=gates, gate_weight=gate_weight, up_weight=up_weight, down_weight=down_weight)


def expert_half(rows, gate_rows, up_rows, down_rows):
    gate_part = lax.dot_general(rows, gate_rows, (((1,), (1,)), ((), ())), preferred_element_type=jnp.float32)
    up_part = lax.dot_general(rows, up_rows, (((1,), (1,)), ((), ())), preferred_element_type=jnp.float32)
    hidden = (jax.nn.silu(gate_part) * up_part).astype(jnp.bfloat16)
    result = jnp.dot(hidden, down_rows, preferred_element_type=jnp.float32)
    return result.astype(jnp.bfloat16)


def reference(tokens, routes, gates, gate_weight, up_weight, down_weight):
    blocks = TOKENS // TOK_DEV
    per_block = routes.reshape(blocks, TOK_DEV * TOP)
    onehot = (per_block[:, :, None] == jnp.arange(EXPERTS, dtype=jnp.int32)[None, None, :]).astype(jnp.int32)
    before = jnp.cumsum(onehot, axis=1) - onehot
    slot_index = jnp.sum(before * onehot, axis=2).astype(jnp.int32)
    position = jnp.arange(blocks, dtype=jnp.int32)[:, None] * CAP + slot_index
    token_index = (jnp.arange(TOKENS * TOP, dtype=jnp.int32) // TOP).reshape(blocks, TOK_DEV * TOP)
    table = jnp.full((EXPERTS, blocks * CAP), TOKENS, jnp.int32).at[per_block, position].set(token_index)
    weight_table = jnp.zeros((EXPERTS, blocks * CAP), gates.dtype).at[per_block, position].set(gates.reshape(blocks, TOK_DEV * TOP))
    half_width = H // 2

    def expert_step(total, expert):
        rows_index = table[expert]
        rows = jnp.take(tokens, rows_index, axis=0, mode="fill", fill_value=0)
        outputs = []
        for which in range(2):
            start = (expert * H + which * half_width).astype(jnp.int32)
            gate_rows = lax.dynamic_slice_in_dim(gate_weight, start, half_width, 0)
            up_rows = lax.dynamic_slice_in_dim(up_weight, start, half_width, 0)
            down_rows = lax.dynamic_slice_in_dim(down_weight, start, half_width, 0)
            outputs.append(expert_half(rows, gate_rows, up_rows, down_rows))
        expert_out = (outputs[0].astype(jnp.float32) + outputs[1].astype(jnp.float32)).astype(jnp.bfloat16)
        contribution = weight_table[expert][:, None].astype(jnp.float32) * expert_out.astype(jnp.float32)
        total = total.at[rows_index].add(contribution, mode="drop")
        return total, None

    total, unused = lax.scan(expert_step, jnp.zeros((TOKENS, D), jnp.float32), jnp.arange(EXPERTS, dtype=jnp.int32))
    return total.astype(jnp.bfloat16)
```

```python
import functools

import jax
import jax.numpy as jnp
from jax import lax
from jax.experimental import pallas as pl
from jax.experimental.pallas import tpu as pltpu
from jax.sharding import PartitionSpec as P

F32 = jnp.float32
BF16 = jnp.bfloat16
MESH = pl.DeviceIdType.MESH


def body(
    tokens, routes, gates, gate_w, up_w, down_w, out,
    slots, rows_in, weights, partial_f, partial_tx, partial_rx, hidden,
    half_tx, half_own, half_rx, summed, returned, comb,
    disp_send, disp_recv, disp_local, fwd_sem,
    ring_send, ring_recv, part_sem, half_sem, ret_send, ret_recv, ret_local,
):
    rep, ep = lax.axis_index("rep"), lax.axis_index("ep")
    z, g = rep // 2, rep % 2
    c, q = ep // 2, ep % 2
    mine = g * 8 + c
    hid_rows, width = gate_w.shape
    half_hid = hid_rows // 2
    half_w = width // 2
    cap = 16
    zs = 8

    def rep_of(z_at, g_at):
        return (z_at % zs) * 2 + g_at

    sibling = {"rep": rep, "ep": c * 2 + 1 - q}
    pair = {"rep": z * 2 + 1 - g, "ep": ep}
    up_z = {"rep": rep_of(z + 1, g), "ep": ep}
    down_z = {"rep": rep_of(z + zs - 1, g), "ep": ep}

    def plane(number):
        return {"rep": z * 2 + number // 8, "ep": (number % 8) * 2 + q}

    barrier = pltpu.get_barrier_semaphore()
    for peer in (sibling, up_z, down_z):
        pl.semaphore_signal(barrier, inc=1, device_id=peer, device_id_type=MESH)

    def greet(k, carry):
        pl.semaphore_signal(
            barrier, inc=1, device_id=plane((mine + k) % 16), device_id_type=MESH
        )
        return carry

    lax.fori_loop(1, 16, greet, 0)

    def prepare(chunk):
        if chunk < 2:
            at = chunk * half_hid
            weights[chunk, z, :, 0:half_hid] = gate_w[at : at + half_hid, :].T
            weights[chunk, z, :, half_hid:] = up_w[at : at + half_hid, :].T
        else:
            weights[chunk, z, :, :] = down_w[...].T

    prepare(0)
    pl.semaphore_wait(barrier, 18)

    def ring_copy(chunk, step, direction, half):
        at = (z + zs - (step - 1)) % zs if direction == 0 else (z + step - 1) % zs
        ref = weights.at[chunk, at, pl.ds(half * half_w, half_w), :]
        return pltpu.make_async_remote_copy(
            src_ref=ref, dst_ref=ref,
            send_sem=ring_send.at[chunk, step - 1, direction, half],
            recv_sem=ring_recv.at[chunk, step - 1, direction, half],
            device_id=up_z if direction == 0 else down_z, device_id_type=MESH,
        )

    def ring_arrival(chunk, step, direction, half):
        at = (z + zs - step) % zs if direction == 0 else (z + step) % zs
        ref = weights.at[chunk, at, pl.ds(half * half_w, half_w), :]
        pltpu.make_async_remote_copy(
            src_ref=ref, dst_ref=ref,
            send_sem=ring_send.at[chunk, step - 1, direction, half],
            recv_sem=ring_recv.at[chunk, step - 1, direction, half],
            device_id=up_z if direction == 0 else down_z, device_id_type=MESH,
        ).wait_recv()

    def hops(step):
        if step == 4:
            return ((0, 0), (1, 1))
        return ((0, 0), (1, 1), (0, 1), (1, 0))

    def ring_open(chunk):
        for direction, half in hops(1):
            ring_copy(chunk, 1, direction, half).start()

    def ring_step(chunk, step):
        for direction, half in hops(step):
            ring_arrival(chunk, step, direction, half)
            if step < 3 or (step == 3 and direction == half):
                ring_copy(chunk, step + 1, direction, half).start()

    ring_open(0)

    lane = lax.broadcasted_iota(jnp.int32, (32, 128), 1)
    expert_of, slot_of = lane // cap, lane % cap
    first = routes[:, 0:1] == expert_of
    second = routes[:, 1:2] == expert_of
    named = jnp.where(first | second, 1.0, 0.0).astype(BF16)
    earlier = jnp.where(
        lax.broadcasted_iota(jnp.int32, (32, 32), 1) < lax.broadcasted_iota(jnp.int32, (32, 32), 0),
        1.0, 0.0,
    ).astype(BF16)
    before = jnp.dot(earlier, named, preferred_element_type=F32)
    taken = (first | second) & (before == slot_of.astype(F32))
    send_map = jnp.where(taken, 1.0, 0.0).astype(BF16)
    comb_map = jnp.where(
        taken, jnp.where(first, gates[:, 0:1], 0.0) + jnp.where(second, gates[:, 1:2], 0.0), 0.0
    )
    comb[0] = comb_map.astype(BF16)
    rest = comb_map - comb[0].astype(F32)
    comb[1] = rest.astype(BF16)
    comb[2] = (rest - comb[1].astype(F32)).astype(BF16)

    for a in range(4):
        block = tokens[:, a * 4 * width : (a + 1) * 4 * width]
        for parity in range(2):
            packed = jnp.concatenate(
                [
                    block[:, parity * width : (parity + 1) * width],
                    block[:, (parity + 2) * width : (parity + 3) * width],
                ],
                axis=1,
            )
            slots[parity * 128 : (parity + 1) * 128, a * 2 * width : (a + 1) * 2 * width] = (
                lax.dot_general(
                    send_map, packed, (((0,), (0,)), ((), ())), preferred_element_type=F32
                ).astype(BF16)
            )

    def rows_of(number):
        return pl.ds(pl.multiple_of(number * cap, cap), cap)

    def disp_copy(k):
        to = (mine + k) % 16
        return pltpu.make_async_remote_copy(
            src_ref=slots.at[rows_of(to), :],
            dst_ref=rows_in.at[q, rows_of(mine), :],
            send_sem=disp_send, recv_sem=disp_recv,
            device_id=plane(to), device_id_type=MESH,
        )

    def disp_start(k, carry):
        disp_copy(k).start()
        return carry

    lax.fori_loop(1, 16, disp_start, 0)
    own_rows = pltpu.make_async_copy(
        slots.at[rows_of(mine), :], rows_in.at[q, rows_of(mine), :], disp_local
    )
    own_rows.start()
    prepare(1)
    prepare(2)

    ring_step(0, 1)

    forward = pltpu.make_async_remote_copy(
        src_ref=rows_in.at[q], dst_ref=rows_in.at[q],
        send_sem=fwd_sem.at[0], recv_sem=fwd_sem.at[1],
        device_id=sibling, device_id_type=MESH,
    )

    ring_step(0, 2)
    own_rows.wait()
    arrived = rows_in.at[q, pl.ds(0, 15 * cap), :]
    pltpu.make_async_copy(arrived, arrived, disp_recv).wait()
    forward.start()
    ring_step(0, 3)
    ring_open(1)
    ring_step(0, 4)
    forward.wait_send()
    pltpu.make_async_remote_copy(
        src_ref=rows_in.at[1 - q], dst_ref=rows_in.at[1 - q],
        send_sem=fwd_sem.at[0], recv_sem=fwd_sem.at[1],
        device_id=sibling, device_id_type=MESH,
    ).wait_recv()

    def part_copy(chunk):
        return pltpu.make_async_remote_copy(
            src_ref=partial_tx.at[chunk], dst_ref=partial_rx.at[chunk],
            send_sem=part_sem.at[0, chunk], recv_sem=part_sem.at[1, chunk],
            device_id=pair, device_id_type=MESH,
        )

    def project(chunk):
        for side in range(2):
            def block(a, total):
                cols = pl.ds(pl.multiple_of(a * 2 * width, 128), 2 * width)
                w = weights[chunk, pl.ds(2 * a, 2)].reshape(2 * width, hid_rows)
                return total + jnp.dot(
                    rows_in[side, :, cols], w, preferred_element_type=F32
                )

            total = lax.fori_loop(0, 4, block, jnp.zeros((256, hid_rows), F32))
            partial_f[chunk, side] = total
            partial_tx[chunk, side] = total.astype(BF16)
        part_copy(chunk).start()

    def activate(chunk):
        part_copy(chunk).wait()
        for side in range(2):
            both = partial_f[chunk, side] + partial_rx[chunk, side].astype(F32)
            gate_part, up_part = both[:, :half_hid], both[:, half_hid:]
            hidden[side, :, chunk * half_hid : (chunk + 1) * half_hid] = (
                gate_part / (1.0 + jnp.exp(-gate_part)) * up_part
            ).astype(BF16)

    project(0)
    ring_step(1, 1)
    ring_step(1, 2)
    ring_step(1, 3)
    ring_open(2)
    activate(0)
    ring_step(1, 4)
    project(1)

    sign = 2 * (z % 2) - 1
    pairs = (z // 2, (z // 2 + 4 + sign) % 4, (z // 2 + 4 - sign) % 4, (z // 2 + 2) % 4)

    def half_copy(s):
        return pltpu.make_async_remote_copy(
            src_ref=half_tx.at[s], dst_ref=half_rx.at[s],
            send_sem=half_sem.at[0, s], recv_sem=half_sem.at[1, s],
            device_id=sibling, device_id_type=MESH,
        )

    def ret_copy(s, k):
        to = (mine + k) % 16
        return pltpu.make_async_remote_copy(
            src_ref=summed.at[s, rows_of(to), :],
            dst_ref=returned.at[s, rows_of(mine), :],
            send_sem=ret_send.at[s], recv_sem=ret_recv.at[s],
            device_id=plane(to), device_id_type=MESH,
        )

    def ret_own(s):
        return pltpu.make_async_copy(
            summed.at[s, rows_of(mine), :], returned.at[s, rows_of(mine), :], ret_local.at[s]
        )

    def lower(s):
        w = weights[2, pl.ds(2 * pairs[s], 2)].reshape(2 * width, hid_rows)
        dims = (((1,), (1,)), ((), ()))
        half_tx[s] = lax.dot_general(
            hidden[1 - q], w, dims, preferred_element_type=F32
        ).astype(BF16)
        half_copy(s).start()
        half_own[...] = lax.dot_general(
            hidden[q], w, dims, preferred_element_type=F32
        ).astype(BF16)
        half_copy(s).wait()
        summed[s] = (half_own[...].astype(F32) + half_rx[s].astype(F32)).astype(BF16)

        def send(k, carry):
            ret_copy(s, k).start()
            return carry

        lax.fori_loop(1, 16, send, 0)
        ret_own(s).start()

    ring_step(2, 1)
    ring_step(2, 2)
    ring_step(2, 3)
    activate(1)
    lower(0)
    lower(1)
    lower(2)
    ring_step(2, 4)
    lower(3)

    def finish(s):
        ret_own(s).wait()
        there = returned.at[s, pl.ds(0, 15 * cap), :]
        pltpu.make_async_copy(there, there, ret_recv.at[s]).wait()
        sums = []
        for parity in range(2):
            block = returned[s, parity * 128 : (parity + 1) * 128, :]
            sums.append(
                (
                    jnp.dot(comb[0], block, preferred_element_type=F32)
                    + jnp.dot(comb[1], block, preferred_element_type=F32)
                    + jnp.dot(comb[2], block, preferred_element_type=F32)
                ).astype(BF16)
            )
        whole = jnp.concatenate(
            [sums[0][:, :width], sums[1][:, :width], sums[0][:, width:], sums[1][:, width:]], axis=1
        )
        out[:, pl.ds(pl.multiple_of(pairs[s] * 4 * width, 128), 4 * width)] = whole

    for s in range(4):
        finish(s)

    sent = slots.at[pl.ds(0, 15 * cap), :]
    pltpu.make_async_copy(sent, sent, disp_send).wait()
    for s in range(4):
        sent = summed.at[s, pl.ds(0, 15 * cap), :]
        pltpu.make_async_copy(sent, sent, ret_send.at[s]).wait()
    for chunk in range(3):
        for step in range(1, 5):
            for direction, half in hops(step):
                ring_copy(chunk, step, direction, half).wait_send()


def per_device(tokens, routes, gates, gate_weight, up_weight, down_weight):
    tok_rows, model = tokens.shape
    hid_rows, width = gate_weight.shape
    vmem = pl.BlockSpec(memory_space=pltpu.VMEM)
    dma = pltpu.SemaphoreType.DMA
    return pl.pallas_call(
        body,
        out_shape=jax.ShapeDtypeStruct((tok_rows, model), BF16),
        in_specs=[vmem] * 6,
        out_specs=vmem,
        scratch_shapes=[
            pltpu.VMEM((256, model // 2), BF16),
            pltpu.VMEM((2, 256, model // 2), BF16),
            pltpu.VMEM((3, 8, width, hid_rows), BF16),
            pltpu.VMEM((2, 2, 256, hid_rows), F32),
            pltpu.VMEM((2, 2, 256, hid_rows), BF16),
            pltpu.VMEM((2, 2, 256, hid_rows), BF16),
            pltpu.VMEM((2, 256, hid_rows), BF16),
            pltpu.VMEM((4, 256, 2 * width), BF16),
            pltpu.VMEM((256, 2 * width), BF16),
            pltpu.VMEM((4, 256, 2 * width), BF16),
            pltpu.VMEM((4, 256, 2 * width), BF16),
            pltpu.VMEM((4, 256, 2 * width), BF16),
            pltpu.VMEM((3, 32, 128), BF16),
            dma, dma, dma, dma((2,)),
            dma((3, 4, 2, 2)), dma((3, 4, 2, 2)), dma((2, 2)), dma((2, 4)),
            dma((4,)), dma((4,)), dma((4,)),
        ],
        compiler_params=pltpu.CompilerParams(
            collective_id=0, has_side_effects=True, vmem_limit_bytes=58 << 20
        ),
    )(tokens, routes, gates, gate_weight, up_weight, down_weight)


def solution(mesh):
    placed = (
        P(("rep", "ep"), None),
        P(("rep", "ep"), None),
        P(("rep", "ep"), None),
        P("ep", "rep"),
        P("ep", "rep"),
        P("ep", "rep"),
    )
    return jax.shard_map(
        per_device, mesh=mesh, in_specs=placed, out_specs=P(("rep", "ep"), None), check_vma=False
    )
```

```python
import functools

import jax
import jax.numpy as jnp
from jax import lax
from jax.experimental import pallas as pl
from jax.experimental.pallas import tpu as pltpu
from jax.sharding import PartitionSpec as P

F32 = jnp.float32
BF16 = jnp.bfloat16
MESH = pl.DeviceIdType.MESH


HIDS = (384, 128)


def body(
    tokens, routes, gates, gate_w, up_w, down_w, out,
    tok, slots, rows_in, w_first, w_second, w_down, part_f0, part_f1, part_tx0, part_tx1,
    part_rx0, part_rx1, hidden, half_tx, half_own, half_rx, summed, returned, comb,
    load_sem, disp_send, disp_recv, disp_local, fwd_sem,
    ring_send, ring_recv, part_sem, half_sem, ret_send, ret_recv, ret_local,
):
    rep, ep = lax.axis_index("rep"), lax.axis_index("ep")
    z, g = rep // 2, rep % 2
    c, q = ep // 2, ep % 2
    mine = g * 8 + c
    width, hid_rows = gate_w.shape
    half_w = width // 2
    cap = 16
    zs = 8
    chunks = (w_first, w_second, w_down)
    part_f, part_tx, part_rx = (part_f0, part_f1), (part_tx0, part_tx1), (part_rx0, part_rx1)

    def rep_of(z_at, g_at):
        return (z_at % zs) * 2 + g_at

    sibling = {"rep": rep, "ep": c * 2 + 1 - q}
    pair = {"rep": z * 2 + 1 - g, "ep": ep}
    up_z = {"rep": rep_of(z + 1, g), "ep": ep}
    down_z = {"rep": rep_of(z + zs - 1, g), "ep": ep}

    def plane(number):
        return {"rep": z * 2 + number // 8, "ep": (number % 8) * 2 + q}

    first, second = HIDS
    loads = [
        pltpu.make_async_copy(src, dst, load_sem.at[i])
        for i, (src, dst) in enumerate((
            (gate_w.at[:, 0:first], w_first.at[z, :, 0:first]),
            (up_w.at[:, 0:first], w_first.at[z, :, first : 2 * first]),
            (tokens, tok),
            (gate_w.at[:, first:], w_second.at[z, :, 0:second]),
            (up_w.at[:, first:], w_second.at[z, :, second : 2 * second]),
            (down_w, w_down.at[z]),
        ))
    ]
    for load in loads:
        load.start()

    barrier = pltpu.get_barrier_semaphore()
    for peer in (sibling, up_z, down_z):
        pl.semaphore_signal(barrier, inc=1, device_id=peer, device_id_type=MESH)

    def greet(k, carry):
        pl.semaphore_signal(
            barrier, inc=1, device_id=plane((mine + k) % 16), device_id_type=MESH
        )
        return carry

    lax.fori_loop(1, 16, greet, 0)
    loads[0].wait()
    loads[1].wait()
    pl.semaphore_wait(barrier, 18)

    def ring_move(chunk, step, direction, half, at):
        ref = chunks[chunk].at[at, pl.ds(half * half_w, half_w), :]
        return pltpu.make_async_remote_copy(
            src_ref=ref, dst_ref=ref,
            send_sem=ring_send.at[chunk, step - 1, direction, half],
            recv_sem=ring_recv.at[chunk, step - 1, direction, half],
            device_id=up_z if direction == 0 else down_z, device_id_type=MESH,
        )

    def ring_copy(chunk, step, direction, half):
        at = (z + zs - (step - 1)) % zs if direction == 0 else (z + step - 1) % zs
        return ring_move(chunk, step, direction, half, at)

    def ring_arrival(chunk, step, direction, half):
        at = (z + zs - step) % zs if direction == 0 else (z + step) % zs
        ring_move(chunk, step, direction, half, at).wait_recv()

    def hops(step):
        if step == 4:
            return ((0, 0), (1, 1))
        return ((0, 0), (1, 1), (0, 1), (1, 0))

    def ring_open(chunk):
        for direction, half in hops(1):
            ring_copy(chunk, 1, direction, half).start()

    def ring_step(chunk, step):
        for direction, half in hops(step):
            ring_arrival(chunk, step, direction, half)
            if step < 3 or (step == 3 and direction == half):
                ring_copy(chunk, step + 1, direction, half).start()

    ring_open(0)

    slot = lax.broadcasted_iota(jnp.int32, (128, 32), 0)
    expert_of, slot_of = slot // cap, slot % cap
    top = routes[0:1, :] == expert_of
    other = routes[1:2, :] == expert_of
    named = jnp.where(top | other, 1.0, 0.0).astype(BF16)
    earlier = jnp.where(
        lax.broadcasted_iota(jnp.int32, (32, 32), 0) < lax.broadcasted_iota(jnp.int32, (32, 32), 1),
        1.0, 0.0,
    ).astype(BF16)
    before = jnp.dot(named, earlier, preferred_element_type=F32)
    taken = (top | other) & (before == slot_of.astype(F32))
    send_map = jnp.where(taken, 1.0, 0.0).astype(BF16)
    comb_map = jnp.where(
        taken, jnp.where(top, gates[0:1, :], 0.0) + jnp.where(other, gates[1:2, :], 0.0), 0.0
    )
    comb[0] = comb_map.astype(BF16)
    rest = comb_map - comb[0].astype(F32)
    comb[1] = rest.astype(BF16)
    comb[2] = (rest - comb[1].astype(F32)).astype(BF16)

    loads[2].wait()
    for a in range(4):
        block = tok[:, a * 4 * width : (a + 1) * 4 * width]
        for parity in range(2):
            packed = jnp.concatenate(
                [
                    block[:, parity * width : (parity + 1) * width],
                    block[:, (parity + 2) * width : (parity + 3) * width],
                ],
                axis=1,
            )
            slots[parity * 128 : (parity + 1) * 128, a * 2 * width : (a + 1) * 2 * width] = (
                jnp.dot(send_map, packed, preferred_element_type=F32).astype(BF16)
            )

    def rows_of(number):
        return pl.ds(pl.multiple_of(number * cap, cap), cap)

    def disp_copy(k):
        to = (mine + k) % 16
        return pltpu.make_async_remote_copy(
            src_ref=slots.at[rows_of(to), :],
            dst_ref=rows_in.at[q, rows_of(mine), :],
            send_sem=disp_send, recv_sem=disp_recv,
            device_id=plane(to), device_id_type=MESH,
        )

    def disp_start(k, carry):
        disp_copy(k).start()
        return carry

    lax.fori_loop(1, 16, disp_start, 0)
    own_rows = pltpu.make_async_copy(
        slots.at[rows_of(mine), :], rows_in.at[q, rows_of(mine), :], disp_local
    )
    own_rows.start()
    for load in loads[3:]:
        load.wait()

    def forward(side):
        return pltpu.make_async_remote_copy(
            src_ref=rows_in.at[side], dst_ref=rows_in.at[side],
            send_sem=fwd_sem.at[0], recv_sem=fwd_sem.at[1],
            device_id=sibling, device_id_type=MESH,
        )

    def part_copy(chunk):
        return pltpu.make_async_remote_copy(
            src_ref=part_tx[chunk], dst_ref=part_rx[chunk],
            send_sem=part_sem.at[0, chunk], recv_sem=part_sem.at[1, chunk],
            device_id=pair, device_id_type=MESH,
        )

    def project(chunk):
        for side in range(2):
            for a in range(4):
                w = chunks[chunk][2 * a : 2 * a + 2].reshape(2 * width, 2 * HIDS[chunk])
                term = jnp.dot(
                    rows_in[side, :, a * 2 * width : (a + 1) * 2 * width], w,
                    preferred_element_type=F32,
                )
                if a == 0:
                    part_f[chunk][side] = term
                else:
                    part_f[chunk][side] += term
            part_tx[chunk][side] = part_f[chunk][side].astype(BF16)
        part_copy(chunk).start()

    def activate(chunk):
        part_copy(chunk).wait()
        n = HIDS[chunk]
        at = sum(HIDS[:chunk])
        for side in range(2):
            both = part_f[chunk][side] + part_rx[chunk][side].astype(F32)
            gate_part, up_part = both[:, :n], both[:, n:]
            hidden[side, :, at : at + n] = (
                gate_part / (1.0 + jnp.exp(-gate_part)) * up_part
            ).astype(BF16)

    sign = 2 * (z % 2) - 1
    pairs = (z // 2, (z // 2 + 4 + sign) % 4, (z // 2 + 4 - sign) % 4, (z // 2 + 2) % 4)

    def half_copy(s):
        return pltpu.make_async_remote_copy(
            src_ref=half_tx.at[s], dst_ref=half_rx.at[s],
            send_sem=half_sem.at[0, s], recv_sem=half_sem.at[1, s],
            device_id=sibling, device_id_type=MESH,
        )

    def ret_copy(s, k):
        to = (mine + k) % 16
        return pltpu.make_async_remote_copy(
            src_ref=summed.at[s, rows_of(to), :],
            dst_ref=returned.at[s, rows_of(mine), :],
            send_sem=ret_send.at[s], recv_sem=ret_recv.at[s],
            device_id=plane(to), device_id_type=MESH,
        )

    def ret_own(s):
        return pltpu.make_async_copy(
            summed.at[s, rows_of(mine), :], returned.at[s, rows_of(mine), :], ret_local.at[s]
        )

    def lower(s):
        w = w_down[pl.ds(2 * pairs[s], 2)].reshape(2 * width, hid_rows)
        dims = (((1,), (1,)), ((), ()))
        half_tx[s] = lax.dot_general(
            hidden[1 - q], w, dims, preferred_element_type=F32
        ).astype(BF16)
        half_copy(s).start()
        half_own[...] = lax.dot_general(
            hidden[q], w, dims, preferred_element_type=F32
        ).astype(BF16)

    def give_back(s):
        half_copy(s).wait()
        summed[s] = (half_own[...].astype(F32) + half_rx[s].astype(F32)).astype(BF16)

        def send(k, carry):
            ret_copy(s, k).start()
            return carry

        lax.fori_loop(1, 16, send, 0)
        ret_own(s).start()

    def finish(s):
        ret_own(s).wait()
        there = returned.at[s, pl.ds(0, 15 * cap), :]
        pltpu.make_async_copy(there, there, ret_recv.at[s]).wait()
        dims = (((0,), (0,)), ((), ()))
        sums = []
        for parity in range(2):
            block = returned[s, parity * 128 : (parity + 1) * 128, :]
            sums.append(
                (
                    lax.dot_general(comb[0], block, dims, preferred_element_type=F32)
                    + lax.dot_general(comb[1], block, dims, preferred_element_type=F32)
                    + lax.dot_general(comb[2], block, dims, preferred_element_type=F32)
                ).astype(BF16)
            )
        whole = jnp.concatenate(
            [sums[0][:, :width], sums[1][:, :width], sums[0][:, width:], sums[1][:, width:]], axis=1
        )
        out[:, pl.ds(pl.multiple_of(pairs[s] * 4 * width, 128), 4 * width)] = whole

    ring_step(0, 1)
    ring_step(0, 2)
    own_rows.wait()
    arrived = rows_in.at[q, pl.ds(0, 15 * cap), :]
    pltpu.make_async_copy(arrived, arrived, disp_recv).wait()
    forward(q).start()
    ring_step(0, 3)
    ring_open(1)
    ring_step(0, 4)
    forward(q).wait_send()
    forward(1 - q).wait_recv()
    project(0)
    ring_step(1, 1)
    ring_step(1, 2)
    ring_step(1, 3)
    ring_open(2)
    ring_step(1, 4)
    project(1)
    activate(0)
    ring_step(2, 1)
    activate(1)
    lower(0)
    give_back(0)
    ring_step(2, 2)
    lower(1)
    give_back(1)
    finish(0)
    ring_step(2, 3)
    lower(2)
    give_back(2)
    ring_step(2, 4)
    lower(3)
    give_back(3)
    finish(1)
    finish(2)
    finish(3)

    sent = slots.at[pl.ds(0, 15 * cap), :]
    pltpu.make_async_copy(sent, sent, disp_send).wait()
    for s in range(4):
        sent = summed.at[s, pl.ds(0, 15 * cap), :]
        pltpu.make_async_copy(sent, sent, ret_send.at[s]).wait()
    for chunk in range(3):
        for step in range(1, 5):
            for direction, half in hops(step):
                ring_copy(chunk, step, direction, half).wait_send()


def per_device(tokens, routes, gates, gate_weight, up_weight, down_weight):
    tok_rows, model = tokens.shape
    hid_rows, width = gate_weight.shape
    vmem = pl.BlockSpec(memory_space=pltpu.VMEM)
    hbm = pl.BlockSpec(memory_space=pltpu.HBM)
    dma = pltpu.SemaphoreType.DMA
    first, second = HIDS
    return pl.pallas_call(
        body,
        out_shape=jax.ShapeDtypeStruct((tok_rows, model), BF16),
        in_specs=[hbm, vmem, vmem, hbm, hbm, hbm],
        out_specs=vmem,
        scratch_shapes=[
            pltpu.VMEM((tok_rows, model), BF16),
            pltpu.VMEM((256, model // 2), BF16),
            pltpu.VMEM((2, 256, model // 2), BF16),
            pltpu.VMEM((8, width, 2 * first), BF16),
            pltpu.VMEM((8, width, 2 * second), BF16),
            pltpu.VMEM((8, width, hid_rows), BF16),
            pltpu.VMEM((2, 256, 2 * first), F32),
            pltpu.VMEM((2, 256, 2 * second), F32),
            pltpu.VMEM((2, 256, 2 * first), BF16),
            pltpu.VMEM((2, 256, 2 * second), BF16),
            pltpu.VMEM((2, 256, 2 * first), BF16),
            pltpu.VMEM((2, 256, 2 * second), BF16),
            pltpu.VMEM((2, 256, hid_rows), BF16),
            pltpu.VMEM((4, 256, 2 * width), BF16),
            pltpu.VMEM((256, 2 * width), BF16),
            pltpu.VMEM((4, 256, 2 * width), BF16),
            pltpu.VMEM((4, 256, 2 * width), BF16),
            pltpu.VMEM((4, 256, 2 * width), BF16),
            pltpu.VMEM((3, 128, 32), BF16),
            dma((6,)), dma, dma, dma, dma((2,)),
            dma((3, 4, 2, 2)), dma((3, 4, 2, 2)), dma((2, 2)), dma((2, 4)),
            dma((4,)), dma((4,)), dma((4,)),
        ],
        compiler_params=pltpu.CompilerParams(
            collective_id=0, has_side_effects=True, vmem_limit_bytes=56 << 20
        ),
    )(tokens, routes.T, gates.T, gate_weight.T, up_weight.T, down_weight.T)


def solution(mesh):
    placed = (
        P(("rep", "ep"), None),
        P(("rep", "ep"), None),
        P(("rep", "ep"), None),
        P("ep", "rep"),
        P("ep", "rep"),
        P("ep", "rep"),
    )
    return jax.shard_map(
        per_device, mesh=mesh, in_specs=placed, out_specs=P(("rep", "ep"), None), check_vma=False
    )
```

```python
import functools

import jax
import jax.numpy as jnp
from jax import lax
from jax.experimental import pallas as pl
from jax.experimental.pallas import tpu as pltpu
from jax.sharding import PartitionSpec as P

F32 = jnp.float32
BF16 = jnp.bfloat16
MESH = pl.DeviceIdType.MESH


HIDS = (256, 128, 128)
COLS = (320, 128)
AROUND = (
    (2, 2), (-1, 2), (2, -1), (1, 2), (2, 1), (0, 2), (2, 0), (-1, 1), (1, -1), (-1, -1), (1, 1),
    (0, -1), (-1, 0), (0, 1), (1, 0),
)


def body(
    tokens, routes, gates, gate_w, up_w, down_w, out,
    tok, slots, rows_in, w0, w1, w2, w3, w4,
    part_f0, part_f1, part_f2, part_tx0, part_tx1, part_tx2, part_rx0, part_rx1, part_rx2,
    hidden, half_tx_a, half_tx_b, half_own_a, half_own_b, half_rx_a, half_rx_b,
    summed_a, summed_b, returned_a, returned_b, sums_a, comb,
    load_sem, disp_send, disp_recv, disp_local, fwd_sem,
    ring_send, ring_recv, part_sem, half_sem, ret_send, ret_recv, ret_local,
):
    rep, ep = lax.axis_index("rep"), lax.axis_index("ep")
    z, g = rep // 2, rep % 2
    c, q = ep // 2, ep % 2
    mine = g * 8 + c
    width, hid_rows = gate_w.shape
    cap = 16
    zs = 8
    chunks = (w0, w1, w2, w3, w4)
    part_f = (part_f0, part_f1, part_f2)
    part_tx = (part_tx0, part_tx1, part_tx2)
    part_rx = (part_rx0, part_rx1, part_rx2)
    half_tx, half_own, half_rx = (half_tx_a, half_tx_b), (half_own_a, half_own_b), (half_rx_a, half_rx_b)
    summed, returned = (summed_a, summed_b), (returned_a, returned_b)

    def rep_of(z_at, g_at):
        return (z_at % zs) * 2 + g_at

    sibling = {"rep": rep, "ep": c * 2 + 1 - q}
    pair = {"rep": z * 2 + 1 - g, "ep": ep}
    up_z = {"rep": rep_of(z + 1, g), "ep": ep}
    down_z = {"rep": rep_of(z + zs - 1, g), "ep": ep}

    def plane(number):
        return {"rep": z * 2 + number // 8, "ep": (number % 8) * 2 + q}

    moves, at = [], 0
    for chunk, n in enumerate(HIDS):
        moves.append((gate_w.at[:, at : at + n], chunks[chunk].at[z, :, 0:n]))
        moves.append((up_w.at[:, at : at + n], chunks[chunk].at[z, :, n : 2 * n]))
        if chunk == 0:
            moves.append((tokens, tok))
        at += n
    moves.append((down_w.at[0 : COLS[0], :], w3.at[z]))
    moves.append((down_w.at[COLS[0] :, :], w4.at[z]))
    loads = [
        pltpu.make_async_copy(src, dst, load_sem.at[i]) for i, (src, dst) in enumerate(moves)
    ]
    for load in loads:
        load.start()

    barrier = pltpu.get_barrier_semaphore()
    for peer in (sibling, up_z, down_z):
        pl.semaphore_signal(barrier, inc=1, device_id=peer, device_id_type=MESH)

    def greet(k, carry):
        pl.semaphore_signal(
            barrier, inc=1, device_id=plane((mine + k) % 16), device_id_type=MESH
        )
        return carry

    lax.fori_loop(1, 16, greet, 0)
    loads[0].wait()
    loads[1].wait()
    pl.semaphore_wait(barrier, 18)

    def ring_move(chunk, step, direction, half, at):
        half_w = chunks[chunk].shape[1] // 2
        ref = chunks[chunk].at[at, pl.ds(half * half_w, half_w), :]
        return pltpu.make_async_remote_copy(
            src_ref=ref, dst_ref=ref,
            send_sem=ring_send.at[chunk, step - 1, direction, half],
            recv_sem=ring_recv.at[chunk, step - 1, direction, half],
            device_id=up_z if direction == 0 else down_z, device_id_type=MESH,
        )

    def ring_copy(chunk, step, direction, half):
        at = (z + zs - (step - 1)) % zs if direction == 0 else (z + step - 1) % zs
        return ring_move(chunk, step, direction, half, at)

    def ring_arrival(chunk, step, direction, half):
        at = (z + zs - step) % zs if direction == 0 else (z + step) % zs
        ring_move(chunk, step, direction, half, at).wait_recv()

    def hops(step):
        if step == 4:
            return ((0, 0), (1, 1))
        return ((0, 0), (1, 1), (0, 1), (1, 0))

    def ring_step(chunk, step):
        for direction, half in hops(step):
            ring_arrival(chunk, step, direction, half)
            if step < 3 or (step == 3 and direction == half):
                ring_copy(chunk, step + 1, direction, half).start()
            if step == 3 and chunk < len(chunks) - 1:
                ring_copy(chunk + 1, 1, direction, half).start()

    for direction, half in hops(1):
        ring_copy(0, 1, direction, half).start()

    slot = lax.broadcasted_iota(jnp.int32, (128, 32), 0)
    expert_of, slot_of = slot // cap, slot % cap
    top = routes[0:1, :] == expert_of
    other = routes[1:2, :] == expert_of
    named = jnp.where(top | other, 1.0, 0.0).astype(BF16)
    earlier = jnp.where(
        lax.broadcasted_iota(jnp.int32, (32, 32), 0) < lax.broadcasted_iota(jnp.int32, (32, 32), 1),
        1.0, 0.0,
    ).astype(BF16)
    before = jnp.dot(named, earlier, preferred_element_type=F32)
    taken = (top | other) & (before == slot_of.astype(F32))
    send_map = jnp.where(taken, 1.0, 0.0).astype(BF16)
    comb_map = jnp.where(
        taken, jnp.where(top, gates[0:1, :], 0.0) + jnp.where(other, gates[1:2, :], 0.0), 0.0
    )
    high = comb_map.astype(BF16)
    rest = comb_map - high.astype(F32)
    middle = rest.astype(BF16)
    low = (rest - middle.astype(F32)).astype(BF16)
    comb[...] = jnp.concatenate([high, middle, low], axis=1)

    loads[2].wait()
    for a in range(4):
        block = tok[:, a * 4 * width : (a + 1) * 4 * width]
        for parity in range(2):
            packed = jnp.concatenate(
                [
                    block[:, parity * width : (parity + 1) * width],
                    block[:, (parity + 2) * width : (parity + 3) * width],
                ],
                axis=1,
            )
            slots[parity * 128 : (parity + 1) * 128, a * 2 * width : (a + 1) * 2 * width] = (
                jnp.dot(send_map, packed, preferred_element_type=F32).astype(BF16)
            )

    def rows_of(number):
        return pl.ds(pl.multiple_of(number * cap, cap), cap)

    flip = 1 - 2 * q

    def around(dx, dy):
        x_to = (c // 2 + 4 + dx * flip) % 4
        y_to = (g * 2 + c % 2 + 4 + dy * flip) % 4
        return (y_to // 2) * 8 + x_to * 2 + y_to % 2

    for dx, dy in AROUND:
        to = around(dx, dy)
        pltpu.make_async_remote_copy(
            src_ref=slots.at[rows_of(to), :],
            dst_ref=rows_in.at[q, rows_of(mine), :],
            send_sem=disp_send, recv_sem=disp_recv,
            device_id=plane(to), device_id_type=MESH,
        ).start()
    own_rows = pltpu.make_async_copy(
        slots.at[rows_of(mine), :], rows_in.at[q, rows_of(mine), :], disp_local
    )
    own_rows.start()
    for load in loads[3:]:
        load.wait()

    def forward(side):
        return pltpu.make_async_remote_copy(
            src_ref=rows_in.at[side], dst_ref=rows_in.at[side],
            send_sem=fwd_sem.at[0], recv_sem=fwd_sem.at[1],
            device_id=sibling, device_id_type=MESH,
        )

    def part_copy(chunk):
        return pltpu.make_async_remote_copy(
            src_ref=part_tx[chunk], dst_ref=part_rx[chunk],
            send_sem=part_sem.at[0, chunk], recv_sem=part_sem.at[1, chunk],
            device_id=pair, device_id_type=MESH,
        )

    def project(chunk):
        for side in range(2):
            for a in range(4):
                w = chunks[chunk][2 * a : 2 * a + 2].reshape(2 * width, 2 * HIDS[chunk])
                term = jnp.dot(
                    rows_in[side, :, a * 2 * width : (a + 1) * 2 * width], w,
                    preferred_element_type=F32,
                )
                if a == 0:
                    part_f[chunk][side] = term
                else:
                    part_f[chunk][side] += term
            part_tx[chunk][side] = part_f[chunk][side].astype(BF16)
        part_copy(chunk).start()

    def activate(chunk):
        part_copy(chunk).wait()
        n = HIDS[chunk]
        at = sum(HIDS[:chunk])
        for side in range(2):
            both = part_f[chunk][side] + part_rx[chunk][side].astype(F32)
            gate_part, up_part = both[:, :n], both[:, n:]
            hidden[side, :, at : at + n] = (
                gate_part / (1.0 + jnp.exp(-gate_part)) * up_part
            ).astype(BF16)

    sign = 2 * (z % 2) - 1
    pairs = (z // 2, (z // 2 + 4 + sign) % 4, (z // 2 + 4 - sign) % 4, (z // 2 + 2) % 4)

    def half_copy(kind, s):
        return pltpu.make_async_remote_copy(
            src_ref=half_tx[kind].at[s], dst_ref=half_rx[kind].at[s],
            send_sem=half_sem.at[0, kind, s], recv_sem=half_sem.at[1, kind, s],
            device_id=sibling, device_id_type=MESH,
        )

    def ret_own(kind, s):
        return pltpu.make_async_copy(
            summed[kind].at[s, rows_of(mine), :], returned[kind].at[s, rows_of(mine), :],
            ret_local.at[kind, s],
        )

    def lower(kind, s):
        w = chunks[3 + kind][pl.ds(2 * pairs[s], 2)].reshape(2 * COLS[kind], hid_rows)
        dims = (((1,), (1,)), ((), ()))
        half_tx[kind][s] = lax.dot_general(
            hidden[1 - q], w, dims, preferred_element_type=F32
        ).astype(BF16)
        half_copy(kind, s).start()
        half_own[kind][s] = lax.dot_general(
            hidden[q], w, dims, preferred_element_type=F32
        ).astype(BF16)

    def give_back(kind, s):
        half_copy(kind, s).wait()
        summed[kind][s] = (
            half_own[kind][s].astype(F32) + half_rx[kind][s].astype(F32)
        ).astype(BF16)
        for dx, dy in AROUND:
            to = around(dx, dy)
            pltpu.make_async_remote_copy(
                src_ref=summed[kind].at[s, rows_of(to), :],
                dst_ref=returned[kind].at[s, rows_of(mine), :],
                send_sem=ret_send.at[kind, s], recv_sem=ret_recv.at[kind, s],
                device_id=plane(to), device_id_type=MESH,
            ).start()
        ret_own(kind, s).start()

    def combine(kind, s):
        ret_own(kind, s).wait()
        there = returned[kind].at[s, pl.ds(0, 15 * cap), :]
        pltpu.make_async_copy(there, there, ret_recv.at[kind, s]).wait()
        dims = (((0,), (0,)), ((), ()))
        sums = []
        for parity in range(2):
            block = returned[kind][s, parity * 128 : (parity + 1) * 128, :]
            terms = lax.dot_general(comb[...], block, dims, preferred_element_type=F32)
            sums.append((terms[0:32] + terms[32:64] + terms[64:96]).astype(BF16))
        return sums

    def finish_a(s):
        for parity, value in enumerate(combine(0, s)):
            sums_a[s, parity] = value

    def finish_b(s):
        wide, narrow = COLS
        pieces = combine(1, s)
        whole = []
        for which in range(2):
            for parity in range(2):
                whole.append(sums_a[s, parity, :, which * wide : (which + 1) * wide])
                whole.append(pieces[parity][:, which * narrow : (which + 1) * narrow])
        out[:, pl.ds(pl.multiple_of(pairs[s] * 4 * width, 128), 4 * width)] = jnp.concatenate(
            whole, axis=1
        )

    ring_step(0, 1)
    ring_step(0, 2)
    own_rows.wait()
    arrived = rows_in.at[q, pl.ds(0, 15 * cap), :]
    pltpu.make_async_copy(arrived, arrived, disp_recv).wait()
    forward(q).start()
    ring_step(0, 3)
    ring_step(0, 4)
    forward(q).wait_send()
    forward(1 - q).wait_recv()
    project(0)
    ring_step(1, 1)
    ring_step(1, 2)
    ring_step(1, 3)
    ring_step(1, 4)
    project(1)
    activate(0)
    ring_step(2, 1)
    ring_step(2, 2)
    activate(1)
    ring_step(2, 3)
    ring_step(2, 4)
    project(2)
    ring_step(3, 1)
    activate(2)
    lower(0, 0)
    give_back(0, 0)
    ring_step(3, 2)
    lower(0, 1)
    give_back(0, 1)
    ring_step(3, 3)
    lower(0, 2)
    ring_step(3, 4)
    give_back(0, 2)
    lower(0, 3)
    ring_step(4, 1)
    give_back(0, 3)
    ring_step(4, 2)
    lower(1, 0)
    lower(1, 1)
    finish_a(0)
    give_back(1, 0)
    give_back(1, 1)
    ring_step(4, 3)
    lower(1, 2)
    finish_a(1)
    give_back(1, 2)
    ring_step(4, 4)
    lower(1, 3)
    finish_a(2)
    give_back(1, 3)
    finish_a(3)
    for s in range(4):
        finish_b(s)

    sent = slots.at[pl.ds(0, 15 * cap), :]
    pltpu.make_async_copy(sent, sent, disp_send).wait()
    for kind in range(2):
        for s in range(4):
            sent = summed[kind].at[s, pl.ds(0, 15 * cap), :]
            pltpu.make_async_copy(sent, sent, ret_send.at[kind, s]).wait()
    for chunk in range(5):
        for step in range(1, 5):
            for direction, half in hops(step):
                ring_copy(chunk, step, direction, half).wait_send()


def per_device(tokens, routes, gates, gate_weight, up_weight, down_weight):
    tok_rows, model = tokens.shape
    hid_rows, width = gate_weight.shape
    vmem = pl.BlockSpec(memory_space=pltpu.VMEM)
    hbm = pl.BlockSpec(memory_space=pltpu.HBM)
    dma = pltpu.SemaphoreType.DMA
    halves = [pltpu.VMEM((4, 256, 2 * n), BF16) for n in COLS]
    return pl.pallas_call(
        body,
        out_shape=jax.ShapeDtypeStruct((tok_rows, model), BF16),
        in_specs=[hbm, vmem, vmem, hbm, hbm, hbm],
        out_specs=vmem,
        scratch_shapes=[
            pltpu.VMEM((tok_rows, model), BF16),
            pltpu.VMEM((256, model // 2), BF16),
            pltpu.VMEM((2, 256, model // 2), BF16),
            *[pltpu.VMEM((8, width, 2 * n), BF16) for n in HIDS],
            *[pltpu.VMEM((8, n, hid_rows), BF16) for n in COLS],
            *[pltpu.VMEM((2, 256, 2 * n), F32) for n in HIDS],
            *[pltpu.VMEM((2, 256, 2 * n), BF16) for n in HIDS],
            *[pltpu.VMEM((2, 256, 2 * n), BF16) for n in HIDS],
            pltpu.VMEM((2, 256, hid_rows), BF16),
            *halves,
            *halves,
            *halves,
            *halves,
            *halves,
            pltpu.VMEM((4, 2, tok_rows, 2 * COLS[0]), BF16),
            pltpu.VMEM((128, 96), BF16),
            dma((9,)), dma, dma, dma, dma((2,)),
            dma((5, 4, 2, 2)), dma((5, 4, 2, 2)), dma((2, 3)), dma((2, 2, 4)),
            dma((2, 4)), dma((2, 4)), dma((2, 4)),
        ],
        compiler_params=pltpu.CompilerParams(
            collective_id=0, has_side_effects=True, vmem_limit_bytes=54592 << 10
        ),
    )(tokens, routes.T, gates.T, gate_weight.T, up_weight.T, down_weight.T)


def solution(mesh):
    placed = (
        P(("rep", "ep"), None),
        P(("rep", "ep"), None),
        P(("rep", "ep"), None),
        P("ep", "rep"),
        P("ep", "rep"),
        P("ep", "rep"),
    )
    return jax.shard_map(
        per_device, mesh=mesh, in_specs=placed, out_specs=P(("rep", "ep"), None), check_vma=False
    )
```

```python
import functools

import jax
import jax.numpy as jnp
from jax import lax
from jax.experimental import pallas as pl
from jax.experimental.pallas import tpu as pltpu
from jax.sharding import PartitionSpec as P

F32 = jnp.float32
BF16 = jnp.bfloat16
MESH = pl.DeviceIdType.MESH


HIDS = (256, 128, 128)
COLS = (320, 128)
AROUND = (
    (2, 2), (-1, 2), (2, -1), (1, 2), (2, 1), (0, 2), (2, 0), (-1, 1), (1, -1), (-1, -1), (1, 1),
    (0, -1), (-1, 0), (0, 1), (1, 0),
)


def body(
    tokens, routes, gates, gate_w, up_w, down_w, out,
    tok, slots, rows_in, w0, w1, w2, w3, w4,
    part_f0, part_f1, part_f2, part_tx0, part_tx1, part_tx2, part_rx0, part_rx1, part_rx2,
    hidden, half_tx_a, half_tx_b, half_own_a, half_own_b, half_rx_a, half_rx_b,
    summed_a, summed_b, returned_a, returned_b, sums_a, comb,
    load_sem, disp_send, disp_recv, disp_local, fwd_sem,
    ring_send, ring_recv, part_sem, half_sem, ret_send, ret_recv, ret_local,
):
    rep, ep = lax.axis_index("rep"), lax.axis_index("ep")
    z, g = rep // 2, rep % 2
    c, q = ep // 2, ep % 2
    mine = g * 8 + c
    width, hid_rows = gate_w.shape
    cap = 16
    zs = 8
    chunks = (w0, w1, w2, w3, w4)
    part_f = (part_f0, part_f1, part_f2)
    part_tx = (part_tx0, part_tx1, part_tx2)
    part_rx = (part_rx0, part_rx1, part_rx2)
    half_tx, half_own, half_rx = (half_tx_a, half_tx_b), (half_own_a, half_own_b), (half_rx_a, half_rx_b)
    summed, returned = (summed_a, summed_b), (returned_a, returned_b)

    def rep_of(z_at, g_at):
        return (z_at % zs) * 2 + g_at

    sibling = {"rep": rep, "ep": c * 2 + 1 - q}
    pair = {"rep": z * 2 + 1 - g, "ep": ep}
    flip = 1 - 2 * q
    up_z = {"rep": rep_of(z + zs + flip, g), "ep": ep}
    down_z = {"rep": rep_of(z + zs - flip, g), "ep": ep}

    def plane(number):
        return {"rep": z * 2 + number // 8, "ep": (number % 8) * 2 + q}

    moves, at = [], 0
    for chunk, n in enumerate(HIDS):
        moves.append((gate_w.at[:, at : at + n], chunks[chunk].at[z, :, 0:n]))
        moves.append((up_w.at[:, at : at + n], chunks[chunk].at[z, :, n : 2 * n]))
        if chunk == 0:
            moves.append((tokens, tok))
        at += n
    moves.append((down_w.at[0 : COLS[0], :], w3.at[z]))
    moves.append((down_w.at[COLS[0] :, :], w4.at[z]))
    loads = [
        pltpu.make_async_copy(src, dst, load_sem.at[i]) for i, (src, dst) in enumerate(moves)
    ]
    for load in loads:
        load.start()

    barrier = pltpu.get_barrier_semaphore()
    for peer in (sibling, up_z, down_z):
        pl.semaphore_signal(barrier, inc=1, device_id=peer, device_id_type=MESH)

    def greet(k, carry):
        pl.semaphore_signal(
            barrier, inc=1, device_id=plane((mine + k) % 16), device_id_type=MESH
        )
        return carry

    lax.fori_loop(1, 16, greet, 0)
    loads[0].wait()
    loads[1].wait()
    pl.semaphore_wait(barrier, 18)

    def ring_move(chunk, step, direction, half, at):
        half_w = chunks[chunk].shape[1] // 2
        ref = chunks[chunk].at[at, pl.ds(half * half_w, half_w), :]
        return pltpu.make_async_remote_copy(
            src_ref=ref, dst_ref=ref,
            send_sem=ring_send.at[chunk, step - 1, direction, half],
            recv_sem=ring_recv.at[chunk, step - 1, direction, half],
            device_id=up_z if direction == 0 else down_z, device_id_type=MESH,
        )

    def ring_copy(chunk, step, direction, half):
        at = (z + zs + (2 * direction - 1) * flip * (step - 1)) % zs
        return ring_move(chunk, step, direction, half, at)

    def ring_arrival(chunk, step, direction, half):
        at = (z + zs + (2 * direction - 1) * flip * step) % zs
        ring_move(chunk, step, direction, half, at).wait_recv()

    def hops(step):
        if step == 4:
            return ((0, 0), (1, 1))
        return ((0, 0), (1, 1), (0, 1), (1, 0))

    def ring_step(chunk, step):
        for direction, half in hops(step):
            ring_arrival(chunk, step, direction, half)
            if step < 3 or (step == 3 and direction == half):
                ring_copy(chunk, step + 1, direction, half).start()
            if step == 3 and chunk < len(chunks) - 1:
                ring_copy(chunk + 1, 1, direction, half).start()

    for direction, half in hops(1):
        ring_copy(0, 1, direction, half).start()

    slot = lax.broadcasted_iota(jnp.int32, (128, 32), 0)
    expert_of, slot_of = slot // cap, slot % cap
    top = routes[0:1, :] == expert_of
    other = routes[1:2, :] == expert_of
    named = jnp.where(top | other, 1.0, 0.0).astype(BF16)
    earlier = jnp.where(
        lax.broadcasted_iota(jnp.int32, (32, 32), 0) < lax.broadcasted_iota(jnp.int32, (32, 32), 1),
        1.0, 0.0,
    ).astype(BF16)
    before = jnp.dot(named, earlier, preferred_element_type=F32)
    taken = (top | other) & (before == slot_of.astype(F32))
    send_map = jnp.where(taken, 1.0, 0.0).astype(BF16)
    comb_map = jnp.where(
        taken, jnp.where(top, gates[0:1, :], 0.0) + jnp.where(other, gates[1:2, :], 0.0), 0.0
    )
    high = comb_map.astype(BF16)
    rest = comb_map - high.astype(F32)
    middle = rest.astype(BF16)
    low = (rest - middle.astype(F32)).astype(BF16)
    comb[...] = jnp.concatenate([high, middle, low], axis=1)

    loads[2].wait()
    for a in range(4):
        block = tok[:, a * 4 * width : (a + 1) * 4 * width]
        for parity in range(2):
            packed = jnp.concatenate(
                [
                    block[:, parity * width : (parity + 1) * width],
                    block[:, (parity + 2) * width : (parity + 3) * width],
                ],
                axis=1,
            )
            slots[parity * 128 : (parity + 1) * 128, a * 2 * width : (a + 1) * 2 * width] = (
                jnp.dot(send_map, packed, preferred_element_type=F32).astype(BF16)
            )

    def rows_of(number):
        return pl.ds(pl.multiple_of(number * cap, cap), cap)

    def around(dx, dy):
        x_to = (c // 2 + 4 + dx * flip) % 4
        y_to = (g * 2 + c % 2 + 4 + dy * flip) % 4
        return (y_to // 2) * 8 + x_to * 2 + y_to % 2

    for dx, dy in AROUND:
        to = around(dx, dy)
        pltpu.make_async_remote_copy(
            src_ref=slots.at[rows_of(to), :],
            dst_ref=rows_in.at[q, rows_of(mine), :],
            send_sem=disp_send, recv_sem=disp_recv,
            device_id=plane(to), device_id_type=MESH,
        ).start()
    own_rows = pltpu.make_async_copy(
        slots.at[rows_of(mine), :], rows_in.at[q, rows_of(mine), :], disp_local
    )
    own_rows.start()
    for load in loads[3:]:
        load.wait()

    def forward(side):
        return pltpu.make_async_remote_copy(
            src_ref=rows_in.at[side], dst_ref=rows_in.at[side],
            send_sem=fwd_sem.at[0], recv_sem=fwd_sem.at[1],
            device_id=sibling, device_id_type=MESH,
        )

    def part_copy(chunk):
        return pltpu.make_async_remote_copy(
            src_ref=part_tx[chunk], dst_ref=part_rx[chunk],
            send_sem=part_sem.at[0, chunk], recv_sem=part_sem.at[1, chunk],
            device_id=pair, device_id_type=MESH,
        )

    def project(chunk):
        for side in range(2):
            for a in range(4):
                w = chunks[chunk][2 * a : 2 * a + 2].reshape(2 * width, 2 * HIDS[chunk])
                term = jnp.dot(
                    rows_in[side, :, a * 2 * width : (a + 1) * 2 * width], w,
                    preferred_element_type=F32,
                )
                if a == 0:
                    part_f[chunk][side] = term
                else:
                    part_f[chunk][side] += term
            part_tx[chunk][side] = part_f[chunk][side].astype(BF16)
        part_copy(chunk).start()

    def activate(chunk):
        part_copy(chunk).wait()
        n = HIDS[chunk]
        at = sum(HIDS[:chunk])
        for side in range(2):
            both = part_f[chunk][side] + part_rx[chunk][side].astype(F32)
            gate_part, up_part = both[:, :n], both[:, n:]
            hidden[side, :, at : at + n] = (
                gate_part / (1.0 + jnp.exp(-gate_part)) * up_part
            ).astype(BF16)

    sign = 2 * (z % 2) - 1
    pairs = (z // 2, (z // 2 + 4 + sign) % 4, (z // 2 + 4 - sign) % 4, (z // 2 + 2) % 4)

    def half_copy(kind, s):
        return pltpu.make_async_remote_copy(
            src_ref=half_tx[kind].at[s], dst_ref=half_rx[kind].at[s],
            send_sem=half_sem.at[0, kind, s], recv_sem=half_sem.at[1, kind, s],
            device_id=sibling, device_id_type=MESH,
        )

    def ret_own(kind, s):
        return pltpu.make_async_copy(
            summed[kind].at[s, rows_of(mine), :], returned[kind].at[s, rows_of(mine), :],
            ret_local.at[kind, s],
        )

    def lower(kind, s):
        w = chunks[3 + kind][pl.ds(2 * pairs[s], 2)].reshape(2 * COLS[kind], hid_rows)
        dims = (((1,), (1,)), ((), ()))
        half_tx[kind][s] = lax.dot_general(
            hidden[1 - q], w, dims, preferred_element_type=F32
        ).astype(BF16)
        half_copy(kind, s).start()
        half_own[kind][s] = lax.dot_general(
            hidden[q], w, dims, preferred_element_type=F32
        ).astype(BF16)

    def give_back(kind, s):
        half_copy(kind, s).wait()
        summed[kind][s] = (
            half_own[kind][s].astype(F32) + half_rx[kind][s].astype(F32)
        ).astype(BF16)
        for dx, dy in AROUND:
            to = around(dx, dy)
            pltpu.make_async_remote_copy(
                src_ref=summed[kind].at[s, rows_of(to), :],
                dst_ref=returned[kind].at[s, rows_of(mine), :],
                send_sem=ret_send.at[kind, s], recv_sem=ret_recv.at[kind, s],
                device_id=plane(to), device_id_type=MESH,
            ).start()
        ret_own(kind, s).start()

    def combine(kind, s):
        ret_own(kind, s).wait()
        there = returned[kind].at[s, pl.ds(0, 15 * cap), :]
        pltpu.make_async_copy(there, there, ret_recv.at[kind, s]).wait()
        dims = (((0,), (0,)), ((), ()))
        sums = []
        for parity in range(2):
            block = returned[kind][s, parity * 128 : (parity + 1) * 128, :]
            terms = lax.dot_general(comb[...], block, dims, preferred_element_type=F32)
            sums.append((terms[0:32] + terms[32:64] + terms[64:96]).astype(BF16))
        return sums

    def finish_a(s):
        for parity, value in enumerate(combine(0, s)):
            sums_a[s, parity] = value

    def finish_b(s):
        wide, narrow = COLS
        pieces = combine(1, s)
        whole = []
        for which in range(2):
            for parity in range(2):
                whole.append(sums_a[s, parity, :, which * wide : (which + 1) * wide])
                whole.append(pieces[parity][:, which * narrow : (which + 1) * narrow])
        out[:, pl.ds(pl.multiple_of(pairs[s] * 4 * width, 128), 4 * width)] = jnp.concatenate(
            whole, axis=1
        )

    ring_step(0, 1)
    ring_step(0, 2)
    own_rows.wait()
    arrived = rows_in.at[q, pl.ds(0, 15 * cap), :]
    pltpu.make_async_copy(arrived, arrived, disp_recv).wait()
    forward(q).start()
    ring_step(0, 3)
    ring_step(0, 4)
    forward(q).wait_send()
    forward(1 - q).wait_recv()
    project(0)
    ring_step(1, 1)
    ring_step(1, 2)
    ring_step(1, 3)
    ring_step(1, 4)
    project(1)
    activate(0)
    ring_step(2, 1)
    ring_step(2, 2)
    activate(1)
    ring_step(2, 3)
    ring_step(2, 4)
    project(2)
    ring_step(3, 1)
    activate(2)
    lower(0, 0)
    give_back(0, 0)
    ring_step(3, 2)
    lower(0, 1)
    give_back(0, 1)
    ring_step(3, 3)
    lower(0, 2)
    ring_step(3, 4)
    give_back(0, 2)
    lower(0, 3)
    ring_step(4, 1)
    give_back(0, 3)
    ring_step(4, 2)
    lower(1, 0)
    lower(1, 1)
    ring_step(4, 3)
    give_back(1, 0)
    give_back(1, 1)
    lower(1, 2)
    ring_step(4, 4)
    lower(1, 3)
    finish_a(0)
    give_back(1, 2)
    finish_a(1)
    give_back(1, 3)
    finish_a(2)
    finish_a(3)
    for s in range(4):
        finish_b(s)

    sent = slots.at[pl.ds(0, 15 * cap), :]
    pltpu.make_async_copy(sent, sent, disp_send).wait()
    for kind in range(2):
        for s in range(4):
            sent = summed[kind].at[s, pl.ds(0, 15 * cap), :]
            pltpu.make_async_copy(sent, sent, ret_send.at[kind, s]).wait()
    for chunk in range(5):
        for step in range(1, 5):
            for direction, half in hops(step):
                ring_copy(chunk, step, direction, half).wait_send()


def per_device(tokens, routes, gates, gate_weight, up_weight, down_weight):
    tok_rows, model = tokens.shape
    hid_rows, width = gate_weight.shape
    vmem = pl.BlockSpec(memory_space=pltpu.VMEM)
    hbm = pl.BlockSpec(memory_space=pltpu.HBM)
    dma = pltpu.SemaphoreType.DMA
    halves = [pltpu.VMEM((4, 256, 2 * n), BF16) for n in COLS]
    return pl.pallas_call(
        body,
        out_shape=jax.ShapeDtypeStruct((tok_rows, model), BF16),
        in_specs=[hbm, vmem, vmem, hbm, hbm, hbm],
        out_specs=vmem,
        scratch_shapes=[
            pltpu.VMEM((tok_rows, model), BF16),
            pltpu.VMEM((256, model // 2), BF16),
            pltpu.VMEM((2, 256, model // 2), BF16),
            *[pltpu.VMEM((8, width, 2 * n), BF16) for n in HIDS],
            *[pltpu.VMEM((8, n, hid_rows), BF16) for n in COLS],
            *[pltpu.VMEM((2, 256, 2 * n), F32) for n in HIDS],
            *[pltpu.VMEM((2, 256, 2 * n), BF16) for n in HIDS],
            *[pltpu.VMEM((2, 256, 2 * n), BF16) for n in HIDS],
            pltpu.VMEM((2, 256, hid_rows), BF16),
            *halves,
            *halves,
            *halves,
            *halves,
            *halves,
            pltpu.VMEM((4, 2, tok_rows, 2 * COLS[0]), BF16),
            pltpu.VMEM((128, 96), BF16),
            dma((9,)), dma, dma, dma, dma((2,)),
            dma((5, 4, 2, 2)), dma((5, 4, 2, 2)), dma((2, 3)), dma((2, 2, 4)),
            dma((2, 4)), dma((2, 4)), dma((2, 4)),
        ],
        compiler_params=pltpu.CompilerParams(
            collective_id=0, has_side_effects=True, vmem_limit_bytes=54592 << 10
        ),
    )(tokens, routes.T, gates.T, gate_weight.T, up_weight.T, down_weight.T)


def solution(mesh):
    placed = (
        P(("rep", "ep"), None),
        P(("rep", "ep"), None),
        P(("rep", "ep"), None),
        P("ep", "rep"),
        P("ep", "rep"),
        P("ep", "rep"),
    )
    return jax.shard_map(
        per_device, mesh=mesh, in_specs=placed, out_specs=P(("rep", "ep"), None), check_vma=False
    )
```

```python
import functools

import jax
import jax.numpy as jnp
from jax import lax
from jax.experimental import pallas as pl
from jax.experimental.pallas import tpu as pltpu
from jax.sharding import PartitionSpec as P

F32 = jnp.float32
BF16 = jnp.bfloat16
MESH = pl.DeviceIdType.MESH


HIDS = (256, 128, 128)
COLS = (320, 128)
AROUND = (
    (2, 2), (-1, 2), (2, -1), (1, 2), (2, 1), (0, 2), (2, 0), (-1, 1), (1, -1), (-1, -1), (1, 1),
    (0, -1), (-1, 0), (0, 1), (1, 0),
)


def body(
    tokens, routes, gates, gate_w, up_w, down_w, out,
    tok, slots, rows_in, w0, w1, w2, w3, w4,
    part_f0, part_f1, part_f2, part_tx0, part_tx1, part_tx2, part_rx0, part_rx1, part_rx2,
    hidden, half_tx_a, half_tx_b, half_own_a, half_own_b, half_rx_a, half_rx_b,
    summed_a, summed_b, returned_a, returned_b, sums_a, comb,
    load_sem, disp_send, disp_recv, disp_local, fwd_sem,
    ring_send, ring_recv, part_sem, half_sem, ret_send, ret_recv, ret_local,
):
    rep, ep = lax.axis_index("rep"), lax.axis_index("ep")
    z, g = rep // 2, rep % 2
    c, q = ep // 2, ep % 2
    mine = g * 8 + c
    width, hid_rows = gate_w.shape
    cap = 16
    zs = 8
    chunks = (w0, w1, w2, w3, w4)
    part_f = (part_f0, part_f1, part_f2)
    part_tx = (part_tx0, part_tx1, part_tx2)
    part_rx = (part_rx0, part_rx1, part_rx2)
    half_tx, half_own, half_rx = (half_tx_a, half_tx_b), (half_own_a, half_own_b), (half_rx_a, half_rx_b)
    summed, returned = (summed_a, summed_b), (returned_a, returned_b)

    def rep_of(z_at, g_at):
        return (z_at % zs) * 2 + g_at

    sibling = {"rep": rep, "ep": c * 2 + 1 - q}
    pair = {"rep": z * 2 + 1 - g, "ep": ep}
    flip = 1 - 2 * q
    up_z = {"rep": rep_of(z + zs + flip, g), "ep": ep}
    down_z = {"rep": rep_of(z + zs - flip, g), "ep": ep}

    def plane(number):
        return {"rep": z * 2 + number // 8, "ep": (number % 8) * 2 + q}

    moves, at = [], 0
    for chunk, n in enumerate(HIDS):
        moves.append((gate_w.at[:, at : at + n], chunks[chunk].at[z, :, 0:n]))
        moves.append((up_w.at[:, at : at + n], chunks[chunk].at[z, :, n : 2 * n]))
        if chunk == 0:
            moves.append((tokens, tok))
        at += n
    moves.append((down_w.at[0 : COLS[0], :], w3.at[z]))
    moves.append((down_w.at[COLS[0] :, :], w4.at[z]))
    loads = [
        pltpu.make_async_copy(src, dst, load_sem.at[i]) for i, (src, dst) in enumerate(moves)
    ]
    loads[0].start()
    loads[1].start()

    barrier = pltpu.get_barrier_semaphore()
    for peer in (sibling, up_z, down_z):
        pl.semaphore_signal(barrier, inc=1, device_id=peer, device_id_type=MESH)

    def greet(k, carry):
        pl.semaphore_signal(
            barrier, inc=1, device_id=plane((mine + k) % 16), device_id_type=MESH
        )
        return carry

    lax.fori_loop(1, 16, greet, 0)
    for load in loads[2:]:
        load.start()
    loads[0].wait()
    loads[1].wait()
    pl.semaphore_wait(barrier, 18)

    def ring_move(chunk, step, direction, half, at):
        half_w = chunks[chunk].shape[1] // 2
        ref = chunks[chunk].at[at, pl.ds(half * half_w, half_w), :]
        return pltpu.make_async_remote_copy(
            src_ref=ref, dst_ref=ref,
            send_sem=ring_send.at[chunk, step - 1, direction, half],
            recv_sem=ring_recv.at[chunk, step - 1, direction, half],
            device_id=up_z if direction == 0 else down_z, device_id_type=MESH,
        )

    def ring_copy(chunk, step, direction, half):
        at = (z + zs + (2 * direction - 1) * flip * (step - 1)) % zs
        return ring_move(chunk, step, direction, half, at)

    def ring_arrival(chunk, step, direction, half):
        at = (z + zs + (2 * direction - 1) * flip * step) % zs
        ring_move(chunk, step, direction, half, at).wait_recv()

    def hops(step):
        if step == 4:
            return ((0, 0), (1, 1))
        return ((0, 0), (1, 1), (0, 1), (1, 0))

    def ring_step(chunk, step):
        for direction, half in hops(step):
            ring_arrival(chunk, step, direction, half)
            if step < 3 or (step == 3 and direction == half):
                ring_copy(chunk, step + 1, direction, half).start()
            if step == 3 and chunk < len(chunks) - 1:
                ring_copy(chunk + 1, 1, direction, half).start()

    for direction, half in hops(1):
        ring_copy(0, 1, direction, half).start()

    slot = lax.broadcasted_iota(jnp.int32, (128, 32), 0)
    expert_of, slot_of = slot // cap, slot % cap
    top = routes[0:1, :] == expert_of
    other = routes[1:2, :] == expert_of
    named = jnp.where(top | other, 1.0, 0.0).astype(BF16)
    earlier = jnp.where(
        lax.broadcasted_iota(jnp.int32, (32, 32), 0) < lax.broadcasted_iota(jnp.int32, (32, 32), 1),
        1.0, 0.0,
    ).astype(BF16)
    before = jnp.dot(named, earlier, preferred_element_type=F32)
    taken = (top | other) & (before == slot_of.astype(F32))
    send_map = jnp.where(taken, 1.0, 0.0).astype(BF16)
    comb_map = jnp.where(
        taken, jnp.where(top, gates[0:1, :], 0.0) + jnp.where(other, gates[1:2, :], 0.0), 0.0
    )
    high = comb_map.astype(BF16)
    rest = comb_map - high.astype(F32)
    middle = rest.astype(BF16)
    low = (rest - middle.astype(F32)).astype(BF16)
    comb[...] = jnp.concatenate([high, middle, low], axis=1)

    loads[2].wait()
    for a in range(4):
        block = tok[:, a * 4 * width : (a + 1) * 4 * width]
        for parity in range(2):
            packed = jnp.concatenate(
                [
                    block[:, parity * width : (parity + 1) * width],
                    block[:, (parity + 2) * width : (parity + 3) * width],
                ],
                axis=1,
            )
            slots[parity * 128 : (parity + 1) * 128, a * 2 * width : (a + 1) * 2 * width] = (
                jnp.dot(send_map, packed, preferred_element_type=F32).astype(BF16)
            )

    def rows_of(number):
        return pl.ds(pl.multiple_of(number * cap, cap), cap)

    def around(dx, dy):
        x_to = (c // 2 + 4 + dx * flip) % 4
        y_to = (g * 2 + c % 2 + 4 + dy * flip) % 4
        return (y_to // 2) * 8 + x_to * 2 + y_to % 2

    for dx, dy in AROUND:
        to = around(dx, dy)
        pltpu.make_async_remote_copy(
            src_ref=slots.at[rows_of(to), :],
            dst_ref=rows_in.at[q, rows_of(mine), :],
            send_sem=disp_send, recv_sem=disp_recv,
            device_id=plane(to), device_id_type=MESH,
        ).start()
    own_rows = pltpu.make_async_copy(
        slots.at[rows_of(mine), :], rows_in.at[q, rows_of(mine), :], disp_local
    )
    own_rows.start()
    for load in loads[3:]:
        load.wait()

    def forward(side):
        return pltpu.make_async_remote_copy(
            src_ref=rows_in.at[side], dst_ref=rows_in.at[side],
            send_sem=fwd_sem.at[0], recv_sem=fwd_sem.at[1],
            device_id=sibling, device_id_type=MESH,
        )

    def part_copy(chunk):
        return pltpu.make_async_remote_copy(
            src_ref=part_tx[chunk], dst_ref=part_rx[chunk],
            send_sem=part_sem.at[0, chunk], recv_sem=part_sem.at[1, chunk],
            device_id=pair, device_id_type=MESH,
        )

    def project(chunk):
        for side in range(2):
            for a in range(4):
                w = chunks[chunk][2 * a : 2 * a + 2].reshape(2 * width, 2 * HIDS[chunk])
                term = jnp.dot(
                    rows_in[side, :, a * 2 * width : (a + 1) * 2 * width], w,
                    preferred_element_type=F32,
                )
                if a == 0:
                    part_f[chunk][side] = term
                else:
                    part_f[chunk][side] += term
            part_tx[chunk][side] = part_f[chunk][side].astype(BF16)
        part_copy(chunk).start()

    def activate(chunk):
        part_copy(chunk).wait()
        n = HIDS[chunk]
        at = sum(HIDS[:chunk])
        for side in range(2):
            both = part_f[chunk][side] + part_rx[chunk][side].astype(F32)
            gate_part, up_part = both[:, :n], both[:, n:]
            hidden[side, :, at : at + n] = (
                gate_part / (1.0 + jnp.exp(-gate_part)) * up_part
            ).astype(BF16)

    sign = 2 * (z % 2) - 1
    pairs = (z // 2, (z // 2 + 4 + sign) % 4, (z // 2 + 4 - sign) % 4, (z // 2 + 2) % 4)

    def half_copy(kind, s):
        return pltpu.make_async_remote_copy(
            src_ref=half_tx[kind].at[s], dst_ref=half_rx[kind].at[s],
            send_sem=half_sem.at[0, kind, s], recv_sem=half_sem.at[1, kind, s],
            device_id=sibling, device_id_type=MESH,
        )

    def ret_own(kind, s):
        return pltpu.make_async_copy(
            summed[kind].at[s, rows_of(mine), :], returned[kind].at[s, rows_of(mine), :],
            ret_local.at[kind, s],
        )

    def lower(kind, s):
        w = chunks[3 + kind][pl.ds(2 * pairs[s], 2)].reshape(2 * COLS[kind], hid_rows)
        dims = (((1,), (1,)), ((), ()))
        half_tx[kind][s] = lax.dot_general(
            hidden[1 - q], w, dims, preferred_element_type=F32
        ).astype(BF16)
        half_copy(kind, s).start()
        half_own[kind][s] = lax.dot_general(
            hidden[q], w, dims, preferred_element_type=F32
        ).astype(BF16)

    def give_back(kind, s):
        half_copy(kind, s).wait()
        summed[kind][s] = (
            half_own[kind][s].astype(F32) + half_rx[kind][s].astype(F32)
        ).astype(BF16)
        for dx, dy in AROUND:
            to = around(dx, dy)
            pltpu.make_async_remote_copy(
                src_ref=summed[kind].at[s, rows_of(to), :],
                dst_ref=returned[kind].at[s, rows_of(mine), :],
                send_sem=ret_send.at[kind, s], recv_sem=ret_recv.at[kind, s],
                device_id=plane(to), device_id_type=MESH,
            ).start()
        ret_own(kind, s).start()

    def combine(kind, s):
        ret_own(kind, s).wait()
        there = returned[kind].at[s, pl.ds(0, 15 * cap), :]
        pltpu.make_async_copy(there, there, ret_recv.at[kind, s]).wait()
        dims = (((0,), (0,)), ((), ()))
        sums = []
        for parity in range(2):
            block = returned[kind][s, parity * 128 : (parity + 1) * 128, :]
            terms = lax.dot_general(comb[...], block, dims, preferred_element_type=F32)
            sums.append((terms[0:32] + terms[32:64] + terms[64:96]).astype(BF16))
        return sums

    def finish_a(s):
        for parity, value in enumerate(combine(0, s)):
            sums_a[s, parity] = value

    def finish_b(s):
        wide, narrow = COLS
        pieces = combine(1, s)
        whole = []
        for which in range(2):
            for parity in range(2):
                whole.append(sums_a[s, parity, :, which * wide : (which + 1) * wide])
                whole.append(pieces[parity][:, which * narrow : (which + 1) * narrow])
        out[:, pl.ds(pl.multiple_of(pairs[s] * 4 * width, 128), 4 * width)] = jnp.concatenate(
            whole, axis=1
        )

    def ring_sent(chunk):
        for step in range(1, 5):
            for direction, half in hops(step):
                ring_copy(chunk, step, direction, half).wait_send()

    def ret_sent(kind, s):
        sent = summed[kind].at[s, pl.ds(0, 15 * cap), :]
        pltpu.make_async_copy(sent, sent, ret_send.at[kind, s]).wait()

    ring_step(0, 1)
    ring_step(0, 2)
    own_rows.wait()
    arrived = rows_in.at[q, pl.ds(0, 15 * cap), :]
    pltpu.make_async_copy(arrived, arrived, disp_recv).wait()
    forward(q).start()
    ring_step(0, 3)
    ring_step(0, 4)
    forward(q).wait_send()
    forward(1 - q).wait_recv()
    sent = slots.at[pl.ds(0, 15 * cap), :]
    pltpu.make_async_copy(sent, sent, disp_send).wait()
    project(0)
    ring_step(1, 1)
    ring_step(1, 2)
    ring_step(1, 3)
    ring_step(1, 4)
    project(1)
    activate(0)
    ring_sent(0)
    ring_step(2, 1)
    ring_step(2, 2)
    activate(1)
    ring_sent(1)
    ring_step(2, 3)
    ring_step(2, 4)
    project(2)
    ring_step(3, 1)
    activate(2)
    lower(0, 0)
    give_back(0, 0)
    ring_sent(2)
    ring_step(3, 2)
    lower(0, 1)
    give_back(0, 1)
    finish_a(0)
    ring_step(3, 3)
    lower(0, 2)
    ring_step(3, 4)
    give_back(0, 2)
    lower(0, 3)
    ring_step(4, 1)
    give_back(0, 3)
    lower(1, 0)
    ring_step(4, 2)
    give_back(1, 0)
    lower(1, 1)
    ring_step(4, 3)
    give_back(1, 1)
    lower(1, 2)
    ring_step(4, 4)
    lower(1, 3)
    give_back(1, 2)
    give_back(1, 3)
    finish_a(1)
    finish_a(2)
    finish_a(3)
    ring_sent(3)
    for s in range(4):
        ret_sent(0, s)
    finish_b(0)
    finish_b(1)
    finish_b(2)
    ring_sent(4)
    for s in range(4):
        ret_sent(1, s)
    finish_b(3)


def per_device(tokens, routes, gates, gate_weight, up_weight, down_weight):
    tok_rows, model = tokens.shape
    hid_rows, width = gate_weight.shape
    vmem = pl.BlockSpec(memory_space=pltpu.VMEM)
    hbm = pl.BlockSpec(memory_space=pltpu.HBM)
    dma = pltpu.SemaphoreType.DMA
    halves = [pltpu.VMEM((4, 256, 2 * n), BF16) for n in COLS]
    return pl.pallas_call(
        body,
        out_shape=jax.ShapeDtypeStruct((tok_rows, model), BF16),
        in_specs=[hbm, vmem, vmem, hbm, hbm, hbm],
        out_specs=vmem,
        scratch_shapes=[
            pltpu.VMEM((tok_rows, model), BF16),
            pltpu.VMEM((256, model // 2), BF16),
            pltpu.VMEM((2, 256, model // 2), BF16),
            *[pltpu.VMEM((8, width, 2 * n), BF16) for n in HIDS],
            *[pltpu.VMEM((8, n, hid_rows), BF16) for n in COLS],
            *[pltpu.VMEM((2, 256, 2 * n), F32) for n in HIDS],
            *[pltpu.VMEM((2, 256, 2 * n), BF16) for n in HIDS],
            *[pltpu.VMEM((2, 256, 2 * n), BF16) for n in HIDS],
            pltpu.VMEM((2, 256, hid_rows), BF16),
            *halves,
            *halves,
            *halves,
            *halves,
            *halves,
            pltpu.VMEM((4, 2, tok_rows, 2 * COLS[0]), BF16),
            pltpu.VMEM((128, 96), BF16),
            dma((9,)), dma, dma, dma, dma((2,)),
            dma((5, 4, 2, 2)), dma((5, 4, 2, 2)), dma((2, 3)), dma((2, 2, 4)),
            dma((2, 4)), dma((2, 4)), dma((2, 4)),
        ],
        compiler_params=pltpu.CompilerParams(
            collective_id=0, has_side_effects=True, vmem_limit_bytes=54592 << 10
        ),
    )(tokens, routes.T, gates.T, gate_weight.T, up_weight.T, down_weight.T)


def solution(mesh):
    placed = (
        P(("rep", "ep"), None),
        P(("rep", "ep"), None),
        P(("rep", "ep"), None),
        P("ep", "rep"),
        P("ep", "rep"),
        P("ep", "rep"),
    )
    return jax.shard_map(
        per_device, mesh=mesh, in_specs=placed, out_specs=P(("rep", "ep"), None), check_vma=False
    )
```

```python
import functools

import jax
import jax.numpy as jnp
from jax import lax
from jax.experimental import pallas as pl
from jax.experimental.pallas import tpu as pltpu
from jax.sharding import PartitionSpec as P

F32 = jnp.float32
BF16 = jnp.bfloat16
MESH = pl.DeviceIdType.MESH


HIDS = (256, 128, 128)
COLS = (320, 128)
AROUND = (
    (2, 2), (-1, 2), (2, -1), (1, 2), (2, 1), (0, 2), (2, 0), (-1, 1), (1, -1), (-1, -1), (1, 1),
    (0, -1), (-1, 0), (0, 1), (1, 0),
)


def body(
    tokens, routes, gates, gate_w, up_w, down_w, out,
    tok, slots, rows_in, w0, w1, w2, w3, w4,
    part_f0, part_f1, part_f2, part_tx0, part_tx1, part_tx2, part_rx0, part_rx1, part_rx2,
    hidden, half_tx_a, half_tx_b, half_own_a, half_own_b, half_rx_a, half_rx_b,
    summed_a, summed_b, returned_a, returned_b, sums_a, comb,
    load_sem, disp_send, disp_recv, disp_local, fwd_sem,
    ring_send, ring_recv, part_sem, half_sem, ret_send, ret_recv, ret_local,
):
    rep, ep = lax.axis_index("rep"), lax.axis_index("ep")
    z, g = rep // 2, rep % 2
    c, q = ep // 2, ep % 2
    mine = g * 8 + c
    width, hid_rows = gate_w.shape
    cap = 16
    zs = 8
    chunks = (w0, w1, w2, w3, w4)
    part_f = (part_f0, part_f1, part_f2)
    part_tx = (part_tx0, part_tx1, part_tx2)
    part_rx = (part_rx0, part_rx1, part_rx2)
    half_tx, half_own, half_rx = (half_tx_a, half_tx_b), (half_own_a, half_own_b), (half_rx_a, half_rx_b)
    summed, returned = (summed_a, summed_b), (returned_a, returned_b)

    def rep_of(z_at, g_at):
        return (z_at % zs) * 2 + g_at

    sibling = {"rep": rep, "ep": c * 2 + 1 - q}
    pair = {"rep": z * 2 + 1 - g, "ep": ep}
    flip = 1 - 2 * q
    up_z = {"rep": rep_of(z + zs + flip, g), "ep": ep}
    down_z = {"rep": rep_of(z + zs - flip, g), "ep": ep}

    def plane(number):
        return {"rep": z * 2 + number // 8, "ep": (number % 8) * 2 + q}

    moves, at = [], 0
    for chunk, n in enumerate(HIDS):
        moves.append((gate_w.at[:, at : at + n], chunks[chunk].at[z, :, 0:n]))
        moves.append((up_w.at[:, at : at + n], chunks[chunk].at[z, :, n : 2 * n]))
        if chunk == 0:
            moves.append((tokens, tok))
        at += n
    moves.append((down_w.at[0 : COLS[0], :], w3.at[z]))
    moves.append((down_w.at[COLS[0] :, :], w4.at[z]))
    loads = [
        pltpu.make_async_copy(src, dst, load_sem.at[i]) for i, (src, dst) in enumerate(moves)
    ]
    loads[0].start()
    loads[1].start()

    barrier = pltpu.get_barrier_semaphore()
    for peer in (sibling, up_z, down_z):
        pl.semaphore_signal(barrier, inc=1, device_id=peer, device_id_type=MESH)

    def greet(k, carry):
        pl.semaphore_signal(
            barrier, inc=1, device_id=plane((mine + k) % 16), device_id_type=MESH
        )
        return carry

    lax.fori_loop(1, 16, greet, 0)
    for load in loads[2:]:
        load.start()
    loads[0].wait()
    loads[1].wait()
    pl.semaphore_wait(barrier, 18)

    def ring_move(chunk, step, direction, half, at):
        half_w = chunks[chunk].shape[1] // 2
        ref = chunks[chunk].at[at, pl.ds(half * half_w, half_w), :]
        return pltpu.make_async_remote_copy(
            src_ref=ref, dst_ref=ref,
            send_sem=ring_send.at[chunk, step - 1, direction, half],
            recv_sem=ring_recv.at[chunk, step - 1, direction, half],
            device_id=up_z if direction == 0 else down_z, device_id_type=MESH,
        )

    def ring_copy(chunk, step, direction, half):
        at = (z + zs + (2 * direction - 1) * flip * (step - 1)) % zs
        return ring_move(chunk, step, direction, half, at)

    def ring_arrival(chunk, step, direction, half):
        at = (z + zs + (2 * direction - 1) * flip * step) % zs
        ring_move(chunk, step, direction, half, at).wait_recv()

    def hops(step):
        if step == 4:
            return ((0, 0), (1, 1))
        return ((0, 0), (1, 1), (0, 1), (1, 0))

    def ring_step(chunk, step):
        for direction, half in hops(step):
            ring_arrival(chunk, step, direction, half)
            if step < 3 or (step == 3 and direction == half):
                ring_copy(chunk, step + 1, direction, half).start()
            if step == 3 and chunk < len(chunks) - 1:
                ring_copy(chunk + 1, 1, direction, half).start()

    for direction, half in hops(1):
        ring_copy(0, 1, direction, half).start()

    slot = lax.broadcasted_iota(jnp.int32, (128, 32), 0)
    expert_of, slot_of = slot // cap, slot % cap
    top = routes[0:1, :] == expert_of
    other = routes[1:2, :] == expert_of
    named = jnp.where(top | other, 1.0, 0.0).astype(BF16)
    earlier = jnp.where(
        lax.broadcasted_iota(jnp.int32, (32, 32), 0) < lax.broadcasted_iota(jnp.int32, (32, 32), 1),
        1.0, 0.0,
    ).astype(BF16)
    before = jnp.dot(named, earlier, preferred_element_type=F32)
    taken = (top | other) & (before == slot_of.astype(F32))
    send_map = jnp.where(taken, 1.0, 0.0).astype(BF16)
    comb_map = jnp.where(
        taken, jnp.where(top, gates[0:1, :], 0.0) + jnp.where(other, gates[1:2, :], 0.0), 0.0
    )
    high = comb_map.astype(BF16)
    rest = comb_map - high.astype(F32)
    middle = rest.astype(BF16)
    low = (rest - middle.astype(F32)).astype(BF16)
    comb[...] = jnp.concatenate([high, middle, low], axis=1)

    loads[2].wait()
    for a in range(4):
        block = tok[:, a * 4 * width : (a + 1) * 4 * width]
        for parity in range(2):
            packed = jnp.concatenate(
                [
                    block[:, parity * width : (parity + 1) * width],
                    block[:, (parity + 2) * width : (parity + 3) * width],
                ],
                axis=1,
            )
            slots[parity * 128 : (parity + 1) * 128, a * 2 * width : (a + 1) * 2 * width] = (
                jnp.dot(send_map, packed, preferred_element_type=F32).astype(BF16)
            )

    def rows_of(number):
        return pl.ds(pl.multiple_of(number * cap, cap), cap)

    def around(dx, dy):
        x_to = (c // 2 + 4 + dx * flip) % 4
        y_to = (g * 2 + c % 2 + 4 + dy * flip) % 4
        return (y_to // 2) * 8 + x_to * 2 + y_to % 2

    for dx, dy in AROUND:
        to = around(dx, dy)
        pltpu.make_async_remote_copy(
            src_ref=slots.at[rows_of(to), :],
            dst_ref=rows_in.at[q, rows_of(mine), :],
            send_sem=disp_send, recv_sem=disp_recv,
            device_id=plane(to), device_id_type=MESH,
        ).start()
    own_rows = pltpu.make_async_copy(
        slots.at[rows_of(mine), :], rows_in.at[q, rows_of(mine), :], disp_local
    )
    own_rows.start()
    for load in loads[3:]:
        load.wait()

    def forward(side):
        return pltpu.make_async_remote_copy(
            src_ref=rows_in.at[side], dst_ref=rows_in.at[side],
            send_sem=fwd_sem.at[0], recv_sem=fwd_sem.at[1],
            device_id=sibling, device_id_type=MESH,
        )

    def part_copy(chunk):
        return pltpu.make_async_remote_copy(
            src_ref=part_tx[chunk], dst_ref=part_rx[chunk],
            send_sem=part_sem.at[0, chunk], recv_sem=part_sem.at[1, chunk],
            device_id=pair, device_id_type=MESH,
        )

    def project(chunk):
        for side in range(2):
            for a in range(4):
                w = chunks[chunk][2 * a : 2 * a + 2].reshape(2 * width, 2 * HIDS[chunk])
                term = jnp.dot(
                    rows_in[side, :, a * 2 * width : (a + 1) * 2 * width], w,
                    preferred_element_type=F32,
                )
                if a == 0:
                    part_f[chunk][side] = term
                else:
                    part_f[chunk][side] += term
            part_tx[chunk][side] = part_f[chunk][side].astype(BF16)
        part_copy(chunk).start()

    def activate(chunk):
        part_copy(chunk).wait()
        n = HIDS[chunk]
        at = sum(HIDS[:chunk])
        for side in range(2):
            both = part_f[chunk][side] + part_rx[chunk][side].astype(F32)
            gate_part, up_part = both[:, :n], both[:, n:]
            hidden[side, :, at : at + n] = (
                gate_part / (1.0 + jnp.exp(-gate_part)) * up_part
            ).astype(BF16)

    sign = 2 * (z % 2) - 1
    pairs = (z // 2, (z // 2 + 4 + sign) % 4, (z // 2 + 4 - sign) % 4, (z // 2 + 2) % 4)

    def half_copy(kind, s):
        return pltpu.make_async_remote_copy(
            src_ref=half_tx[kind].at[s], dst_ref=half_rx[kind].at[s],
            send_sem=half_sem.at[0, kind, s], recv_sem=half_sem.at[1, kind, s],
            device_id=sibling, device_id_type=MESH,
        )

    def ret_own(kind, s):
        return pltpu.make_async_copy(
            summed[kind].at[s, rows_of(mine), :], returned[kind].at[s, rows_of(mine), :],
            ret_local.at[kind, s],
        )

    def block(kind, s, side):
        w = chunks[3 + kind][pl.ds(2 * pairs[s], 2)].reshape(2 * COLS[kind], hid_rows)
        dims = (((1,), (1,)), ((), ()))
        return lax.dot_general(
            hidden[side], w, dims, preferred_element_type=F32
        ).astype(BF16)

    def lower_other(kind, s):
        half_tx[kind][s] = block(kind, s, 1 - q)
        half_copy(kind, s).start()

    def lower_own(kind, s):
        half_own[kind][s] = block(kind, s, q)

    def lower(kind, s):
        lower_other(kind, s)
        lower_own(kind, s)

    def give_back(kind, s):
        half_copy(kind, s).wait()
        summed[kind][s] = (
            half_own[kind][s].astype(F32) + half_rx[kind][s].astype(F32)
        ).astype(BF16)
        for dx, dy in AROUND:
            to = around(dx, dy)
            pltpu.make_async_remote_copy(
                src_ref=summed[kind].at[s, rows_of(to), :],
                dst_ref=returned[kind].at[s, rows_of(mine), :],
                send_sem=ret_send.at[kind, s], recv_sem=ret_recv.at[kind, s],
                device_id=plane(to), device_id_type=MESH,
            ).start()
        ret_own(kind, s).start()

    def combine(kind, s):
        ret_own(kind, s).wait()
        there = returned[kind].at[s, pl.ds(0, 15 * cap), :]
        pltpu.make_async_copy(there, there, ret_recv.at[kind, s]).wait()
        dims = (((0,), (0,)), ((), ()))
        sums = []
        for parity in range(2):
            block = returned[kind][s, parity * 128 : (parity + 1) * 128, :]
            terms = lax.dot_general(comb[...], block, dims, preferred_element_type=F32)
            sums.append((terms[0:32] + terms[32:64] + terms[64:96]).astype(BF16))
        return sums

    def finish_a(s):
        for parity, value in enumerate(combine(0, s)):
            sums_a[s, parity] = value

    def finish_b(s):
        wide, narrow = COLS
        pieces = combine(1, s)
        whole = []
        for which in range(2):
            for parity in range(2):
                whole.append(sums_a[s, parity, :, which * wide : (which + 1) * wide])
                whole.append(pieces[parity][:, which * narrow : (which + 1) * narrow])
        out[:, pl.ds(pl.multiple_of(pairs[s] * 4 * width, 128), 4 * width)] = jnp.concatenate(
            whole, axis=1
        )

    def ring_sent(chunk):
        for step in range(1, 5):
            for direction, half in hops(step):
                ring_copy(chunk, step, direction, half).wait_send()

    def ret_sent(kind, s):
        sent = summed[kind].at[s, pl.ds(0, 15 * cap), :]
        pltpu.make_async_copy(sent, sent, ret_send.at[kind, s]).wait()

    ring_step(0, 1)
    ring_step(0, 2)
    own_rows.wait()
    arrived = rows_in.at[q, pl.ds(0, 15 * cap), :]
    pltpu.make_async_copy(arrived, arrived, disp_recv).wait()
    forward(q).start()
    ring_step(0, 3)
    ring_step(0, 4)
    forward(q).wait_send()
    forward(1 - q).wait_recv()
    sent = slots.at[pl.ds(0, 15 * cap), :]
    pltpu.make_async_copy(sent, sent, disp_send).wait()
    project(0)
    ring_step(1, 1)
    ring_step(1, 2)
    ring_step(1, 3)
    ring_step(1, 4)
    project(1)
    activate(0)
    ring_sent(0)
    ring_step(2, 1)
    ring_step(2, 2)
    activate(1)
    ring_sent(1)
    ring_step(2, 3)
    ring_step(2, 4)
    project(2)
    ring_step(3, 1)
    activate(2)
    lower(0, 0)
    give_back(0, 0)
    ring_sent(2)
    ring_step(3, 2)
    lower(0, 1)
    give_back(0, 1)
    finish_a(0)
    ring_step(3, 3)
    lower(0, 2)
    ring_step(3, 4)
    lower_other(0, 3)
    give_back(0, 2)
    lower_own(0, 3)
    ring_step(4, 1)
    lower_other(1, 0)
    give_back(0, 3)
    lower_own(1, 0)
    ring_step(4, 2)
    lower_other(1, 1)
    give_back(1, 0)
    lower_own(1, 1)
    ring_step(4, 3)
    lower_other(1, 2)
    give_back(1, 1)
    lower_own(1, 2)
    ring_step(4, 4)
    lower_other(1, 3)
    give_back(1, 2)
    lower_own(1, 3)
    give_back(1, 3)
    finish_a(1)
    finish_a(2)
    finish_a(3)
    ring_sent(3)
    for s in range(4):
        ret_sent(0, s)
    finish_b(0)
    finish_b(1)
    finish_b(2)
    ring_sent(4)
    for s in range(4):
        ret_sent(1, s)
    finish_b(3)


def per_device(tokens, routes, gates, gate_weight, up_weight, down_weight):
    tok_rows, model = tokens.shape
    hid_rows, width = gate_weight.shape
    vmem = pl.BlockSpec(memory_space=pltpu.VMEM)
    hbm = pl.BlockSpec(memory_space=pltpu.HBM)
    dma = pltpu.SemaphoreType.DMA
    halves = [pltpu.VMEM((4, 256, 2 * n), BF16) for n in COLS]
    return pl.pallas_call(
        body,
        out_shape=jax.ShapeDtypeStruct((tok_rows, model), BF16),
        in_specs=[hbm, vmem, vmem, hbm, hbm, hbm],
        out_specs=vmem,
        scratch_shapes=[
            pltpu.VMEM((tok_rows, model), BF16),
            pltpu.VMEM((256, model // 2), BF16),
            pltpu.VMEM((2, 256, model // 2), BF16),
            *[pltpu.VMEM((8, width, 2 * n), BF16) for n in HIDS],
            *[pltpu.VMEM((8, n, hid_rows), BF16) for n in COLS],
            *[pltpu.VMEM((2, 256, 2 * n), F32) for n in HIDS],
            *[pltpu.VMEM((2, 256, 2 * n), BF16) for n in HIDS],
            *[pltpu.VMEM((2, 256, 2 * n), BF16) for n in HIDS],
            pltpu.VMEM((2, 256, hid_rows), BF16),
            *halves,
            *halves,
            *halves,
            *halves,
            *halves,
            pltpu.VMEM((4, 2, tok_rows, 2 * COLS[0]), BF16),
            pltpu.VMEM((128, 96), BF16),
            dma((9,)), dma, dma, dma, dma((2,)),
            dma((5, 4, 2, 2)), dma((5, 4, 2, 2)), dma((2, 3)), dma((2, 2, 4)),
            dma((2, 4)), dma((2, 4)), dma((2, 4)),
        ],
        compiler_params=pltpu.CompilerParams(
            collective_id=0, has_side_effects=True, vmem_limit_bytes=54592 << 10
        ),
    )(tokens, routes.T, gates.T, gate_weight.T, up_weight.T, down_weight.T)


def solution(mesh):
    placed = (
        P(("rep", "ep"), None),
        P(("rep", "ep"), None),
        P(("rep", "ep"), None),
        P("ep", "rep"),
        P("ep", "rep"),
        P("ep", "rep"),
    )
    return jax.shard_map(
        per_device, mesh=mesh, in_specs=placed, out_specs=P(("rep", "ep"), None), check_vma=False
    )
```
